512 devices in a mesh: seq: 64 (over y_lo, z, x), head: 8 (over y_hi, core).
Axes of the slice: x: 4, y: 8 (y_hi: 4, y_lo: 2; y = y_hi * 2 + y_lo), z: 8, core: 2. Of those that a mesh axis runs over, the one named last changes fastest.
Arguments:
- values: bfloat16 [2, 4096, 4096], P(None, 'seq', 'head'), may hold values from -6 to 6
- keys_b: bfloat16 [2, 4096, 128], P(None, 'seq'), may hold values from -0.29882812 to 0.29882812
- queries_c: bfloat16 [2, 4096, 128], P(None, 'seq'), may hold values from -0.29882812 to 0.29882812
- forget: float32 [2, 64, 4096], P(None, 'head', 'seq'), may hold values from 0 to 2
- skip: float32 [64], P('head'), may hold values from 0.5 to 1.5
- cotangent: bfloat16 [2, 4096, 4096], P(None, 'seq', 'head'), may hold values from -0.59765625 to 0.59765625
Outputs:
- mixed: bfloat16 [2, 4096, 4096], P(None, 'seq', 'head')
- grad_values: bfloat16 [2, 4096, 4096], P(None, 'seq', 'head')
- grad_bc: float32 [2, 2, 4096, 128], P(None, None, ('seq', 'head'))
The draws below stay inside these ranges and needn't reach their ends.
All inputs are finite; a program needn't handle non-finite values.
Results may differ from the reference program's by a relative error of at most 0.012.
Values sent between devices are 32-bit elements; how exact they have to be, the bound alone decides.
A program may use at most 128 MiB of HBM per device.

```python
import math
import jax
import jax.numpy as jnp
from jax import lax

HEADS = 64
HEAD_DIM = 64
STATE = 128
SEQS = 2
SEQ_DEV = 64
WIDTH = 4096
LENGTH = 4096


def draw_forget(key, part):
    streams = jax.random.split(key, 6)
    blocks = LENGTH // SEQ_DEV
    slow_share = 0.5
    slow = jax.random.uniform(streams[0], (SEQS, HEADS, 1)) < slow_share
    fast_rate = jnp.exp(jax.random.uniform(streams[1], (SEQS, HEADS, 1), minval=math.log(1.0 / 50.0), maxval=math.log(1.0 / 30.0)))
    forgetting_speed = jnp.where(slow, 0.6 / LENGTH, fast_rate)
    approximate_guess = jnp.exp(jax.random.uniform(streams[2], (SEQS, HEADS, LENGTH), minval=math.log(0.5), maxval=math.log(2.0)))
    processor_factor = jnp.exp(jax.random.uniform(streams[3], (SEQS, 1, blocks, 1), minval=math.log(0.7), maxval=math.log(1.4)))
    processor_factor = jnp.broadcast_to(processor_factor, (SEQS, 1, blocks, SEQ_DEV)).reshape(SEQS, 1, LENGTH)
    probe_locations = jax.random.randint(streams[4], (SEQS, 1, 1, 2), 0, LENGTH)
    recurrence_levels = jax.random.uniform(streams[5], (SEQS, 1, 1, 2), minval=0.25, maxval=0.7)
    token_offset = jnp.arange(LENGTH)[None, None, :, None]
    span_count = jnp.sum(jnp.where(token_offset == probe_locations, recurrence_levels, 0.0), axis=-1)
    return (forgetting_speed * approximate_guess * processor_factor + span_count).astype(jnp.float32)


def levels(stream_key, shape, cuts, least, largest):
    loudness, own = 1.0, jax.random.fold_in(stream_key, 6)
    for dim, blocks in cuts:
        steps = jnp.exp(jax.random.uniform(jax.random.fold_in(own, dim), (blocks,), jnp.float32, least / len(cuts), largest / len(cuts)))
        loudness = loudness * jnp.repeat(steps, shape[dim] // blocks).reshape([-1 if axis == dim else 1 for axis in range(len(shape))])
    return loudness


def gaussian(rng, shape, scale, limit, cuts=(), kind=jnp.bfloat16):
    drawn = jax.random.normal(rng, shape, jnp.float32) * scale
    if len(cuts) > 0:
        drawn = levels(rng, shape, cuts, -0.22, 0.18) * drawn
    return jnp.clip(drawn, min=-limit, max=limit).astype(kind)


def setup_inputs(seed: int = 0) -> dict:
    splits = jax.random.split(jax.random.key(seed), 7)
    return {
        "values": gaussian(splits[0], (SEQS, LENGTH, WIDTH), 1.0, 6.0, ((1, 64), (2, 8))),
        "keys_b": gaussian(splits[1], (SEQS, LENGTH, STATE), 0.05, 0.29882812, ((1, 64),)),
        "queries_c": gaussian(splits[2], (SEQS, LENGTH, STATE), 0.05, 0.29882812, ((1, 64),)),
        "forget": draw_forget(jax.random.fold_in(splits[6], 71), 0),
        "skip": jnp.clip(0.5 + 1.0 * jax.random.uniform(splits[4], (HEADS,), jnp.float32) ** levels(splits[4], (HEADS,), ((0, 8),), -0.2, 0.2), 0.5, 1.5),
        "cotangent": gaussian(splits[5], (SEQS, LENGTH, WIDTH), 0.1, 0.59765625, ((1, 64), (2, 8))),
    }


def own_state(values, keys_wide, logcum):
    seq_count, rows, wide = values.shape
    head_count = logcum.shape[1]
    tail_decay = jnp.exp(logcum[..., -1:] - logcum)
    scaled = values.astype(jnp.float32).reshape(seq_count, rows, head_count, wide // head_count)
    scaled = scaled * jnp.transpose(tail_decay, (0, 2, 1))[..., None]
    return jnp.einsum('suhp,sun->shpn', scaled, keys_wide, precision=lax.Precision.HIGHEST)

def read_state(queries_wide, logcum, carried):
    inner_part = jnp.einsum('stn,shpn->sthp', queries_wide, carried, precision=lax.Precision.HIGHEST)
    return inner_part * jnp.transpose(jnp.exp(logcum), (0, 2, 1))[..., None]

def block_scores(queries_c, keys_b):
    return jnp.einsum('stn,sun->stu', queries_c, keys_b, preferred_element_type=jnp.float32)

def block_pass(values, keys_wide, queries_wide, scores, forget, skip, carried):
    seq_count, rows, wide = values.shape
    head_count = skip.shape[0]
    head_width = wide // head_count
    logcum = jnp.cumsum(-forget, axis=-1)
    causal = jnp.arange(rows)[:, None] >= jnp.arange(rows)[None, :]
    log_gap = logcum[..., :, None] - logcum[..., None, :]
    decay_mask = jnp.where(causal, jnp.exp(jnp.where(causal, log_gap, 0.0)), 0.0)
    weights = (scores[:, None] * decay_mask).astype(jnp.bfloat16)
    by_head = values.reshape(seq_count, rows, head_count, head_width)
    own_part = jnp.einsum('shtu,suhp->sthp', weights, by_head, preferred_element_type=jnp.float32)
    summed = own_part + read_state(queries_wide, logcum, carried) + skip[:, None] * by_head.astype(jnp.float32)
    mixed = summed.reshape(seq_count, rows, wide).astype(jnp.bfloat16)
    final_state = jnp.exp(logcum[..., -1])[..., None, None] * carried + own_state(values, keys_wide, logcum)
    return (mixed, final_state)

def reference(values, keys_b, queries_c, forget, skip, cotangent):
    blocks = LENGTH // SEQ_DEV

    def to_blocks(array):
        return jnp.transpose(array.reshape(SEQS, blocks, SEQ_DEV, array.shape[-1]), (1, 0, 2, 3))

    def from_blocks(array):
        return jnp.transpose(array, (1, 0, 2, 3)).reshape(SEQS, LENGTH, array.shape[-1])
    forget_blocks = jnp.transpose(forget.reshape(SEQS, HEADS, blocks, SEQ_DEV), (2, 0, 1, 3))
    key_blocks = to_blocks(keys_b)
    query_blocks = to_blocks(queries_c)
    score_blocks = lax.map(lambda pair: block_scores(pair[0], pair[1]), (query_blocks, key_blocks))
    key_wide = key_blocks.astype(jnp.float32)
    query_wide = query_blocks.astype(jnp.float32)

    def forward(value_blocks, key_all, query_all, score_all, forget_all):

        def block_step(carried, pieces):
            mixed, final_state = block_pass(pieces[0], pieces[1], pieces[2], pieces[3], pieces[4], skip, carried)
            return (final_state, mixed)
        start = jnp.zeros((SEQS, HEADS, HEAD_DIM, STATE), jnp.float32)
        _, outputs = lax.scan(jax.checkpoint(block_step), start, (value_blocks, key_all, query_all, score_all, forget_all))
        return outputs
    outputs, pullback = jax.vjp(forward, to_blocks(values), key_wide, query_wide, score_blocks, forget_blocks)
    grads = pullback(to_blocks(cotangent))
    score_grad = grads[3]
    grad_query = grads[2] + jnp.einsum('bstu,bsun->bstn', score_grad, key_wide, precision=lax.Precision.HIGHEST)
    grad_key = grads[1] + jnp.einsum('bstu,bstn->bsun', score_grad, query_wide, precision=lax.Precision.HIGHEST)
    mixed = from_blocks(outputs)
    grad_values = from_blocks(grads[0])
    grad_bc = jnp.stack([from_blocks(grad_key), from_blocks(grad_query)])
    return (mixed, grad_values, grad_bc)
```

```python
import functools

import jax
import jax.numpy as jnp
from jax import lax
from jax.experimental import pallas as pl
from jax.experimental.pallas import tpu as pltpu
from jax.sharding import PartitionSpec as P

MESH = pl.DeviceIdType.MESH
GROUP = 4
F32 = jnp.float32
BF16 = jnp.bfloat16


def dot(a, b):
    return lax.dot_general(a, b, (((1,), (0,)), ((), ())), preferred_element_type=F32)


def dot_nt(a, b):
    return lax.dot_general(a, b, (((1,), (1,)), ((), ())), preferred_element_type=F32)


def dot_tn(a, b):
    return lax.dot_general(a, b, (((0,), (0,)), ((), ())), preferred_element_type=F32)


def iota(shape, dim):
    return lax.broadcasted_iota(jnp.int32, shape, dim)


def kernel(
    sizes,
    values_ref, keys_ref, queries_ref, forget_ref, skip_ref, cot_ref,
    mixed_ref, gv_ref, gbc_ref,
    e_head, e_tail, s_val, s_cot, mix_acc, gv_acc, bc_acc,
    dx_send, dx_recv, dz_send, dz_recv,
    xin_send, xin_recv, zin_send, zin_recv, zout_send, zout_recv, xout_send, xout_recv,
    rs_send, rs_recv,
    send_sem, recv_sem,
):
    groups, peers = sizes
    seqs, rows, wide = values_ref.shape
    heads = forget_ref.shape[1]
    width = wide // heads
    state = keys_ref.shape[2]
    lanes = wide // GROUP
    piece = state // groups
    part = rows // peers
    streams = 2 * seqs

    me_seq = lax.axis_index("seq")
    me_head = lax.axis_index("head")
    me_x = lax.rem(me_seq, GROUP)
    me_g = me_seq // GROUP

    def x_peer(k):
        x = lax.rem(me_x + k, GROUP)
        return x, (me_g * GROUP + x, me_head)

    def z_peer(k):
        g = lax.rem(me_g + k, groups)
        return g, (g * GROUP + me_x, me_head)

    def h_peer(k):
        h = lax.rem(me_head + k, peers)
        return h, (me_seq, h)

    barrier = pltpu.get_barrier_semaphore()
    for peer, count in ((x_peer, GROUP), (z_peer, groups), (h_peer, peers)):
        for k in range(1, count):
            pl.semaphore_signal(barrier, 1, device_id=peer(k)[1], device_id_type=MESH)

    def copy(src, dst, slot, target):
        return pltpu.make_async_remote_copy(
            src_ref=src, dst_ref=dst, send_sem=send_sem.at[slot], recv_sem=recv_sem.at[slot],
            device_id=target, device_id_type=MESH,
        )

    def slot_of(phase, q):
        return 2 + phase * streams + q

    def spread(peer, count, src, dst, slot):
        for k in range(1, count):
            index, target = peer(k)
            copy(src(index), dst, slot, target).start()

    def arrived(buffer, count, slot):
        view = buffer.at[pl.ds(0, count - 1)]
        copy(view, view, slot, (me_seq, me_head)).wait_recv()

    def sent(buffer, count, slot):
        view = buffer.at[pl.ds(0, count - 1)]
        copy(view, view, slot, (me_seq, me_head)).wait_send()

    spread_heads = (iota((heads, wide), 1) // width == iota((heads, wide), 0)).astype(BF16)
    row2, col2 = iota((2 * rows, 2 * rows), 0), iota((2 * rows, 2 * rows), 1)
    upto = jnp.where(
        row2 < rows,
        (lax.rem(col2, rows) <= row2).astype(F32),
        (lax.rem(col2, rows) > row2 - rows).astype(F32),
    ).astype(BF16)
    row_w, lane_w = iota((rows, wide), 0), lax.rem(iota((rows, wide), 1), width)

    def decays(s):
        f = forget_ref[s]
        high = f.astype(BF16)
        low = (f - high.astype(F32)).astype(BF16)
        return dot_tn(high, spread_heads), dot_tn(low, spread_heads)

    fx = []
    for s in range(seqs):
        high, low = decays(s)
        fx.append((high, low))
        both = jnp.concatenate([high, low], axis=0).astype(BF16)
        sums = dot(upto, both)
        e_head[s] = jnp.exp(-sums[:rows])
        e_tail[s] = jnp.exp(-sums[rows:])
        total = jnp.exp(-sums[rows - 1 : rows])
        for j in range(GROUP):
            dx_send[j, s * 4 : s * 4 + 4] = jnp.broadcast_to(
                total[:, j * lanes : (j + 1) * lanes], (4, lanes)
            )
    dx_recv[me_x] = dx_send[me_x]
    pl.semaphore_wait(barrier, (GROUP - 1) + (groups - 1) + (peers - 1))
    spread(x_peer, GROUP, lambda i: dx_send.at[i], dx_recv.at[me_x], 0)
    for s in range(seqs):
        for back in range(2):
            q = 2 * s + back
            if back:
                scaled = (cot_ref[s].astype(F32) * e_head[s]).astype(BF16)
                s_cot[s] = scaled
                local = dot_tn(queries_ref[s], scaled)
            else:
                scaled = (values_ref[s].astype(F32) * e_tail[s]).astype(BF16)
                s_val[s] = scaled
                local = dot_tn(keys_ref[s], scaled)
            for j in range(GROUP):
                xin_send[q, j] = local[:, j * lanes : (j + 1) * lanes]
            spread(x_peer, GROUP, lambda i: xin_send.at[q, i], xin_recv.at[q, me_x], slot_of(0, q))
            xin_recv[q, me_x] = xin_send[q, me_x]

    def local_work(s):
        high, low = fx[s]
        zero = jnp.zeros((rows, wide), F32)

        def gap(keep, half):
            picked = jnp.concatenate(
                [jnp.where(keep, high, zero), jnp.where(keep, low, zero)], axis=0
            ).astype(BF16)
            return jnp.exp(-dot(half, picked))

        decay = jnp.where(lane_w <= row_w, gap(row_w > lane_w, upto[:rows]), 0.0)
        decay_t = jnp.where(lane_w >= row_w, gap(row_w <= lane_w, upto[rows:]), 0.0)
        keys, queries = keys_ref[s], queries_ref[s]
        keys2 = jnp.concatenate([keys, keys], axis=0)
        queries2 = jnp.concatenate([queries, queries], axis=0)
        copies = wide // (2 * rows)
        scores = jnp.concatenate([dot_nt(queries, keys2)] * copies, axis=1)
        scores_t = jnp.concatenate([dot_nt(keys, queries2)] * copies, axis=1)
        weights = (scores * decay).astype(BF16)
        weights_t = (scores_t * decay_t).astype(BF16)
        quad = 4 * width
        mask = (iota((quad, quad), 0) // rows == iota((quad, quad), 1) // width).astype(BF16)
        grad_sum = None
        for c in range(wide // quad):
            cols = slice(c * quad, (c + 1) * quad)
            val, cot = values_ref[s, :, cols], cot_ref[s, :, cols]
            val_diag = jnp.concatenate([val] * 4, axis=0) * mask
            cot_diag = jnp.concatenate([cot] * 4, axis=0) * mask
            skip_row = jnp.concatenate(
                [
                    jnp.where(
                        iota((1, 2 * width), 1) < width,
                        skip_ref[0, 4 * c + 2 * i],
                        skip_ref[0, 4 * c + 2 * i + 1],
                    )
                    for i in range(2)
                ],
                axis=1,
            )
            mix_acc[s, :, cols] = dot(weights[:, cols], val_diag) + skip_row * val.astype(F32)
            gv_acc[s, :, cols] = dot(weights_t[:, cols], cot_diag) + skip_row * cot.astype(F32)
            grad_w = dot_nt(cot, val_diag) * decay[:, cols]
            for i in range(2):
                term = grad_w[:, i * 2 * width : (i + 1) * 2 * width]
                grad_sum = term if grad_sum is None else grad_sum + term
        grad_sum = grad_sum.astype(BF16)
        bc_acc[2 * s] = dot(grad_sum, keys2)
        folded = dot_tn(grad_sum, queries)
        bc_acc[2 * s + 1] = folded[:rows] + folded[rows:]

    def decay_x(s, i):
        return dx_recv[i, 4 * s : 4 * s + 1]

    def decay_z(s, g):
        return dz_recv[g, 4 * s : 4 * s + 1]

    def group_total(q):
        s, back = q // 2, q % 2
        arrived(xin_recv.at[q], GROUP, slot_of(0, q))
        order = range(GROUP - 1, -1, -1) if back else range(GROUP)
        total = None
        for i in order:
            term = xin_recv[q, i]
            total = term if total is None else decay_x(s, i) * total + term
        zin_send[q] = total.reshape(groups, piece, lanes)
        spread(z_peer, groups, lambda g: zin_send.at[q, g], zin_recv.at[q, me_g], slot_of(1, q))
        zin_recv[q, me_g] = zin_send[q, me_g]

    def group_scan(q):
        s, back = q // 2, q % 2
        arrived(zin_recv.at[q], groups, slot_of(1, q))
        order = range(groups - 1, -1, -1) if back else range(groups)
        carry = jnp.zeros((piece, lanes), F32)
        for g in order:
            zout_send[q, g] = carry
            carry = decay_z(s, g) * carry + zin_recv[q, g]
        spread(z_peer, groups, lambda g: zout_send.at[q, g], zout_recv.at[q, me_g], slot_of(2, q))
        zout_recv[q, me_g] = zout_send[q, me_g]

    def member_scan(q):
        s, back = q // 2, q % 2
        arrived(zout_recv.at[q], groups, slot_of(2, q))
        order = range(GROUP - 1, -1, -1) if back else range(GROUP)
        carry = zout_recv[q].reshape(state, lanes)
        for n, i in enumerate(order):
            xout_send[q, i] = carry
            if n < GROUP - 1:
                carry = decay_x(s, i) * carry + xin_recv[q, i]
        spread(x_peer, GROUP, lambda i: xout_send.at[q, i], xout_recv.at[q, me_x], slot_of(3, q))
        xout_recv[q, me_x] = xout_send[q, me_x]

    def finish(q):
        s, back = q // 2, q % 2
        arrived(xout_recv.at[q], GROUP, slot_of(3, q))
        carried = jnp.concatenate([xout_recv[q, j] for j in range(GROUP)], axis=1).astype(BF16)
        if back:
            grad = bc_acc[2 * s + 1] + dot_nt(s_val[s], carried)
        else:
            grad = bc_acc[2 * s] + dot_nt(s_cot[s], carried)
        rs_send[q] = grad.reshape(peers, part, state)
        spread(h_peer, peers, lambda h: rs_send.at[q, h], rs_recv.at[q, me_head], slot_of(4, q))
        rs_recv[q, me_head] = rs_send[q, me_head]
        if back:
            gv_ref[s] = (gv_acc[s] + e_tail[s] * dot(keys_ref[s], carried)).astype(BF16)
        else:
            mixed_ref[s] = (mix_acc[s] + e_head[s] * dot(queries_ref[s], carried)).astype(BF16)

    def reduce_heads(q):
        s, back = q // 2, q % 2
        arrived(rs_recv.at[q], peers, slot_of(4, q))
        total = rs_recv[q, 0]
        for h in range(1, peers):
            total = total + rs_recv[q, h]
        gbc_ref[1 - back, s] = total

    arrived(dx_recv, GROUP, 0)
    product = dx_recv[0]
    for i in range(1, GROUP):
        product = product * dx_recv[i]
    dz_send[...] = product
    spread(z_peer, groups, lambda g: dz_send, dz_recv.at[me_g], 1)
    dz_recv[me_g] = product
    local_work(0)
    group_total(0)
    group_total(1)
    local_work(1)
    arrived(dz_recv, groups, 1)
    group_scan(0)
    group_total(2)
    group_scan(1)
    group_total(3)
    member_scan(0)
    group_scan(2)
    member_scan(1)
    group_scan(3)
    finish(0)
    member_scan(2)
    finish(1)
    member_scan(3)
    finish(2)
    reduce_heads(0)
    reduce_heads(1)
    finish(3)
    reduce_heads(2)
    reduce_heads(3)

    sent(dx_send, GROUP, 0)
    sent(dz_recv, groups, 1)
    for q in range(streams):
        sent(xin_send.at[q], GROUP, slot_of(0, q))
        sent(zin_send.at[q], groups, slot_of(1, q))
        sent(zout_send.at[q], groups, slot_of(2, q))
        sent(xout_send.at[q], GROUP, slot_of(3, q))
        sent(rs_send.at[q], peers, slot_of(4, q))


def solution(mesh):
    blocks, peers = mesh.shape["seq"], mesh.shape["head"]
    groups = blocks // GROUP

    def shards(values, keys_b, queries_c, forget, skip, cotangent):
        seqs, rows, wide = values.shape
        state = keys_b.shape[-1]
        streams = 2 * seqs
        lanes, piece, part = wide // GROUP, state // groups, rows // peers
        slots = 2 + 5 * streams
        vmem = pl.BlockSpec(memory_space=pltpu.VMEM)
        smem = pl.BlockSpec(memory_space=pltpu.SMEM)
        return pl.pallas_call(
            functools.partial(kernel, (groups, peers)),
            out_shape=(
                jax.ShapeDtypeStruct(values.shape, BF16),
                jax.ShapeDtypeStruct(values.shape, BF16),
                jax.ShapeDtypeStruct((2, seqs, part, state), F32),
            ),
            in_specs=[vmem, vmem, vmem, vmem, smem, vmem],
            out_specs=(vmem, vmem, vmem),
            scratch_shapes=[
                pltpu.VMEM((seqs, rows, wide), F32),
                pltpu.VMEM((seqs, rows, wide), F32),
                pltpu.VMEM((seqs, rows, wide), BF16),
                pltpu.VMEM((seqs, rows, wide), BF16),
                pltpu.VMEM((seqs, rows, wide), F32),
                pltpu.VMEM((seqs, rows, wide), F32),
                pltpu.VMEM((2 * seqs, rows, state), F32),
                pltpu.VMEM((GROUP, 4 * seqs, lanes), F32),
                pltpu.VMEM((GROUP, 4 * seqs, lanes), F32),
                pltpu.VMEM((4 * seqs, lanes), F32),
                pltpu.VMEM((groups, 4 * seqs, lanes), F32),
                pltpu.VMEM((streams, GROUP, state, lanes), F32),
                pltpu.VMEM((streams, GROUP, state, lanes), F32),
                pltpu.VMEM((streams, groups, piece, lanes), F32),
                pltpu.VMEM((streams, groups, piece, lanes), F32),
                pltpu.VMEM((streams, groups, piece, lanes), F32),
                pltpu.VMEM((streams, groups, piece, lanes), F32),
                pltpu.VMEM((streams, GROUP, state, lanes), F32),
                pltpu.VMEM((streams, GROUP, state, lanes), F32),
                pltpu.VMEM((streams, peers, part, state), F32),
                pltpu.VMEM((streams, peers, part, state), F32),
                pltpu.SemaphoreType.DMA((slots,)),
                pltpu.SemaphoreType.DMA((slots,)),
            ],
            compiler_params=pltpu.CompilerParams(collective_id=0, has_side_effects=True),
        )(values, keys_b, queries_c, forget, skip.reshape(1, -1), cotangent)

    in_specs = (
        P(None, "seq", "head"),
        P(None, "seq", None),
        P(None, "seq", None),
        P(None, "head", "seq"),
        P("head"),
        P(None, "seq", "head"),
    )
    out_specs = (
        P(None, "seq", "head"),
        P(None, "seq", "head"),
        P(None, None, ("seq", "head"), None),
    )
    return jax.shard_map(shards, mesh=mesh, in_specs=in_specs, out_specs=out_specs, check_vma=False)
```

```python
import functools

import jax
import jax.numpy as jnp
from jax import lax
from jax.experimental import pallas as pl
from jax.experimental.pallas import tpu as pltpu
from jax.sharding import PartitionSpec as P

MESH = pl.DeviceIdType.MESH
GROUP = 4
F32 = jnp.float32
BF16 = jnp.bfloat16


def dot(a, b):
    return lax.dot_general(a, b, (((1,), (0,)), ((), ())), preferred_element_type=F32)


def dot_nt(a, b):
    return lax.dot_general(a, b, (((1,), (1,)), ((), ())), preferred_element_type=F32)


def dot_tn(a, b):
    return lax.dot_general(a, b, (((0,), (0,)), ((), ())), preferred_element_type=F32)


def iota(shape, dim):
    return lax.broadcasted_iota(jnp.int32, shape, dim)


ORDER = (
    ("T", 0), ("T", 1), ("L", 1), ("T", 2), ("T", 3), ("D", 0), ("S", 0), ("T", 4), ("S", 1), ("T", 5),
    ("S", 2), ("T", 6), ("S", 3), ("T", 7), ("M", 0), ("S", 4), ("M", 1), ("S", 5), ("M", 2), ("S", 6),
    ("M", 3), ("S", 7), ("M", 4), ("F", 0), ("M", 5), ("M", 6), ("F", 1), ("M", 7), ("F", 2), ("R", 0),
    ("R", 1), ("F", 3), ("R", 2), ("R", 3),
)


def kernel(
    sizes,
    values_in, keys_in, queries_in, forget_in, skip_in, cot_in,
    mixed_out, gv_out, gbc_out,
    values_ref, keys_ref, queries_ref, forget_ref, skip_ref, cot_ref,
    mixed_ref, gv_ref, gbc_ref,
    e_head, e_tail, s_val, s_cot, mix_acc, gv_acc, bc_acc,
    dx_send, dx_recv, dz_send, dz_recv,
    xin_send, xin_recv, zin_send, zin_recv, zout_send, zout_recv, xout_send, xout_recv,
    rs_send, rs_recv,
    send_sem, recv_sem, load_sem, round_sem, write_sem,
):
    groups, peers = sizes
    seqs, rows, wide = values_ref.shape
    heads = forget_ref.shape[1]
    width = wide // heads
    state = keys_ref.shape[2]
    lanes = wide // GROUP
    half = state // 2
    piece = state // groups
    depth = groups // 2
    part = rows // peers

    me_seq = lax.axis_index("seq")
    me_head = lax.axis_index("head")
    me_x = lax.rem(me_seq, GROUP)
    me_g = me_seq // GROUP
    me_y, me_z = me_g // depth, lax.rem(me_g, depth)
    parity, me_piece = lax.rem(me_g, 2), me_g // 2

    loads = [
        pltpu.make_async_copy(src, dst, load_sem.at[n])
        for n, (src, dst) in enumerate(
            (
                (forget_in, forget_ref), (keys_in, keys_ref), (values_in, values_ref),
                (queries_in, queries_ref), (cot_in, cot_ref), (skip_in, skip_ref),
            )
        )
    ]
    for load in loads:
        load.start()

    def at_x(x):
        return (me_g * GROUP + x, me_head)

    def at_group(g):
        return (g * GROUP + me_x, me_head)

    x_peers = [lax.rem(me_x + k, GROUP) for k in (2, 1, 3)]
    away = sorted(
        ((dy, dz) for dy in range(2) for dz in range(depth) if dy or dz),
        key=lambda d: -(d[0] + min(d[1], depth - d[1])),
    )
    z_peers = [
        lax.rem(me_y + dy, 2) * depth + lax.rem(me_z + dz, depth) for dy, dz in away
    ]
    cores = 2 if peers % 2 == 0 else 1
    ring = peers // cores
    me_r, me_c = me_head // cores, lax.rem(me_head, cores)
    h_away = sorted(
        ((dr, dc) for dr in range(ring) for dc in range(cores) if dr or dc),
        key=lambda d: -min(d[0], ring - d[0]),
    )
    h_peers = [
        lax.rem(me_r + dr, ring) * cores + lax.rem(me_c + dc, cores) for dr, dc in h_away
    ]

    def steps(size, *distances):
        return sorted({d % size for d in distances} - {0})

    def z_near(*distances):
        return [
            at_group(me_y * depth + lax.rem(me_z + d, depth)) for d in steps(depth, *distances)
        ]

    y_other = [at_group((1 - me_y) * depth + me_z)]
    core_other = [(me_seq, me_r * cores + 1 - me_c)] if cores == 2 else []
    h_near = core_other + [
        (me_seq, lax.rem(me_r + d, ring) * cores + me_c) for d in steps(ring, 1, -1)
    ]
    barrier = pltpu.get_barrier_semaphore()
    near = [at_x(x) for x in x_peers] + h_near + y_other + z_near(1, -1)
    for target in near:
        pl.semaphore_signal(barrier, 1, device_id=target, device_id_type=MESH)
    rounds = (z_near(1, -1) + y_other, z_near(2, -2), y_other, h_near, core_other)

    def tell(n):
        for target in rounds[n]:
            pl.semaphore_signal(round_sem.at[n], 1, device_id=target, device_id_type=MESH)

    def told(n):
        if rounds[n]:
            pl.semaphore_wait(round_sem.at[n], len(rounds[n]))

    def copy(src, dst, send, recv, target):
        return pltpu.make_async_remote_copy(
            src_ref=src, dst_ref=dst, send_sem=send_sem.at[send], recv_sem=recv_sem.at[recv],
            device_id=target, device_id_type=MESH,
        )

    streams = 2 * seqs
    X_IN, Z_IN, Z_OUT, X_OUT, HEADS = range(2, 7)
    x_in, z_in, z_out, x_out, heads_in = (
        2, 2 + 2 * streams, 2 + 3 * streams, 2 + 5 * streams, 2 + 6 * streams
    )

    def arrived(view, slot):
        copy(view, view, slot, slot, (me_seq, me_head)).wait_recv()

    def sent(view, slot):
        copy(view, view, slot, slot, (me_seq, me_head)).wait_send()

    every = seqs * wide
    lane_head = iota((seqs * heads, every), 1) // width
    spread_heads = (lane_head == iota((seqs * heads, every), 0)).astype(BF16)
    row2, col2 = iota((2 * rows, 2 * rows), 0), iota((2 * rows, 2 * rows), 1)
    upto = jnp.where(
        row2 < rows,
        (lax.rem(col2, rows) <= row2).astype(F32),
        (lax.rem(col2, rows) > row2 - rows).astype(F32),
    ).astype(BF16)
    row_w, lane_w = iota((rows, wide), 0), lax.rem(iota((rows, wide), 1), width)

    loads[0].wait()
    flat = forget_ref[...].reshape(seqs * heads, rows)
    high = flat.astype(BF16)
    low = (flat - high.astype(F32)).astype(BF16)
    high, low = dot_tn(high, spread_heads), dot_tn(low, spread_heads)
    sums = dot(upto, jnp.concatenate([high, low], axis=0).astype(BF16))
    for s in range(seqs):
        cols = slice(s * wide, (s + 1) * wide)
        e_head[s] = jnp.exp(-sums[:rows, cols])
        e_tail[s] = jnp.exp(-sums[rows:, cols])
        total = jnp.exp(-sums[rows - 1 : rows, cols])
        for j in range(GROUP):
            dx_send[j, s : s + 1] = total[:, j * lanes : (j + 1) * lanes]
    dx_recv[me_x] = dx_send[me_x]

    def local_state(q):
        s, back = q // 2, q % 2
        if back:
            scaled = (cot_ref[s].astype(F32) * e_head[s]).astype(BF16)
            s_cot[s] = scaled
            local = dot_tn(queries_ref[s], scaled)
        else:
            scaled = (values_ref[s].astype(F32) * e_tail[s]).astype(BF16)
            s_val[s] = scaled
            local = dot_tn(keys_ref[s], scaled)
        for j in range(GROUP):
            xin_send[q, j] = local[:, j * lanes : (j + 1) * lanes]

    def half_rows(h):
        return pl.ds(h * half, half)

    def send_state(q):
        for h in range(2):
            for x in x_peers:
                copy(
                    xin_send.at[q, x, half_rows(h)], xin_recv.at[q, me_x, half_rows(h)],
                    X_IN, x_in + 2 * q + h, at_x(x),
                ).start()
        xin_recv[q, me_x] = xin_send[q, me_x]

    loads[1].wait()
    loads[2].wait()
    local_state(0)
    pl.semaphore_wait(barrier, len(near))
    tell(0)
    tell(3)
    for x in x_peers:
        copy(dx_send.at[x], dx_recv.at[me_x], 0, 0, at_x(x)).start()
    send_state(0)
    for load in loads[3:]:
        load.wait()
    for q in range(1, 2 * seqs):
        local_state(q)
        send_state(q)

    def local_work(s):
        mine = slice(s * wide, (s + 1) * wide)
        zero = jnp.zeros((rows, wide), F32)

        def gap(keep, span):
            picked = jnp.concatenate(
                [jnp.where(keep, high[:, mine], zero), jnp.where(keep, low[:, mine], zero)], axis=0
            ).astype(BF16)
            return jnp.exp(-dot(span, picked))

        decay = jnp.where(lane_w <= row_w, gap(row_w > lane_w, upto[:rows]), 0.0)
        decay_t = jnp.where(lane_w >= row_w, gap(row_w <= lane_w, upto[rows:]), 0.0)
        keys, queries = keys_ref[s], queries_ref[s]
        keys2 = jnp.concatenate([keys, keys], axis=0)
        queries2 = jnp.concatenate([queries, queries], axis=0)
        copies = wide // (2 * rows)
        scores = jnp.concatenate([dot_nt(queries, keys2)] * copies, axis=1)
        scores_t = jnp.concatenate([dot_nt(keys, queries2)] * copies, axis=1)
        weights = (scores * decay).astype(BF16)
        weights_t = (scores_t * decay_t).astype(BF16)
        quad = 4 * width
        mask = (iota((quad, quad), 0) // rows == iota((quad, quad), 1) // width).astype(BF16)
        grad_sum = None
        for c in range(wide // quad):
            cols = slice(c * quad, (c + 1) * quad)
            val, cot = values_ref[s, :, cols], cot_ref[s, :, cols]
            val_diag = jnp.concatenate([val] * 4, axis=0) * mask
            cot_diag = jnp.concatenate([cot] * 4, axis=0) * mask
            skip_row = jnp.concatenate(
                [
                    jnp.broadcast_to(skip_ref[0:1, 4 * c + i : 4 * c + i + 1], (1, width))
                    for i in range(4)
                ],
                axis=1,
            )
            mix_acc[s, :, cols] = dot(weights[:, cols], val_diag) + skip_row * val.astype(F32)
            gv_acc[s, :, cols] = dot(weights_t[:, cols], cot_diag) + skip_row * cot.astype(F32)
            grad_w = dot_nt(cot, val_diag) * decay[:, cols]
            for i in range(2):
                term = grad_w[:, i * 2 * width : (i + 1) * 2 * width]
                grad_sum = term if grad_sum is None else grad_sum + term
        grad_sum = grad_sum.astype(BF16)
        bc_acc[2 * s] = dot(grad_sum, keys2)
        folded = dot_tn(grad_sum, queries)
        bc_acc[2 * s + 1] = folded[:rows] + folded[rows:]

    def decay_x(s, i):
        return dx_recv[i, s : s + 1]

    def decay_z(s, g):
        return dz_recv[g, s : s + 1]

    def group_total(q, h):
        s, back = q // 2, q % 2
        arrived(xin_recv.at[q, pl.ds(0, GROUP - 1), half_rows(h)], x_in + 2 * q + h)
        order = range(GROUP - 1, -1, -1) if back else range(GROUP)
        total = None
        for i in order:
            term = xin_recv[q, i, half_rows(h)]
            total = term if total is None else decay_x(s, i) * total + term
        zin_send[q, h] = total.reshape(depth, piece, lanes)
        first = lax.rem(me_z + h, 2)

        def send(dy, k):
            g = lax.rem(me_y + dy, 2) * depth + lax.rem(me_z + first + 2 * k, depth)
            copy(
                zin_send.at[q, h, g // 2], zin_recv.at[q, me_g],
                Z_IN, z_in + q, at_group(g),
            ).start()

        hops = sorted(range(depth // 2), key=lambda k: -min(2 * k + 1, depth - 2 * k))
        for dy, k in [(1, k) for k in hops] + [(0, k) for k in hops if k]:
            send(dy, k)

        @pl.when(parity != h)
        def _():
            send(0, 0)

        @pl.when(parity == h)
        def _():
            zin_recv[q, me_g] = zin_send[q, h, me_piece]

    def group_scan(q, h):
        s, back = q // 2, q % 2

        @pl.when(parity == h)
        def _():
            arrived(zin_recv.at[q, pl.ds(0, groups - 1)], z_in + q)
            order = range(groups - 1, -1, -1) if back else range(groups)
            carry = jnp.zeros((piece, lanes), F32)
            for n, g in enumerate(order):
                zout_send[q, g] = carry
                if n < groups - 1:
                    carry = decay_z(s, g) * carry + zin_recv[q, g]
            for g in z_peers:
                copy(
                    zout_send.at[q, g], zout_recv.at[q, h, me_piece],
                    Z_OUT, z_out + 2 * q + h, at_group(g),
                ).start()
            zout_recv[q, h, me_piece] = zout_send[q, me_g]

    def member_scan(q, h):
        s, back = q // 2, q % 2

        @pl.when(parity != h)
        def _():
            arrived(zout_recv.at[q, h], z_out + 2 * q + h)

        @pl.when(parity == h)
        def _():
            arrived(zout_recv.at[q, h, pl.ds(0, depth - 1)], z_out + 2 * q + h)

        order = range(GROUP - 1, -1, -1) if back else range(GROUP)
        carry = zout_recv[q, h].reshape(half, lanes)
        for n, i in enumerate(order):
            xout_send[q, i, half_rows(h)] = carry
            if n < GROUP - 1:
                carry = decay_x(s, i) * carry + xin_recv[q, i, half_rows(h)]
        for x in x_peers:
            copy(
                xout_send.at[q, x, half_rows(h)], xout_recv.at[q, me_x, half_rows(h)],
                X_OUT, x_out + q, at_x(x),
            ).start()
        xout_recv[q, me_x, half_rows(h)] = xout_send[q, me_x, half_rows(h)]

    written = []

    def finish(q):
        s, back = q // 2, q % 2
        arrived(xout_recv.at[q, pl.ds(0, GROUP - 1)], x_out + q)
        carried = jnp.concatenate([xout_recv[q, j] for j in range(GROUP)], axis=1).astype(BF16)
        if back:
            grad = bc_acc[2 * s + 1] + dot_nt(s_val[s], carried)
        else:
            grad = bc_acc[2 * s] + dot_nt(s_cot[s], carried)
        rs_send[q] = grad.reshape(peers, part, state)
        for p in h_peers:
            copy(
                rs_send.at[q, p], rs_recv.at[q, me_head], HEADS, heads_in + q, (me_seq, p)
            ).start()
        rs_recv[q, me_head] = rs_send[q, me_head]
        if back:
            gv_ref[s] = (gv_acc[s] + e_tail[s] * dot(keys_ref[s], carried)).astype(BF16)
        else:
            mixed_ref[s] = (mix_acc[s] + e_head[s] * dot(queries_ref[s], carried)).astype(BF16)
        source, result = (gv_ref, gv_out) if back else (mixed_ref, mixed_out)
        written.append(pltpu.make_async_copy(source.at[s], result.at[s], write_sem.at[q]))
        written[-1].start()

    def reduce_heads(q):
        s, back = q // 2, q % 2
        arrived(rs_recv.at[q, pl.ds(0, peers - 1)], heads_in + q)
        total = rs_recv[q, 0]
        for h in range(1, peers):
            total = total + rs_recv[q, h]
        gbc_ref[1 - back, s] = total

    local_work(0)
    for n in range(3):
        told(n)
        if n < 2:
            tell(n + 1)
    told(3)
    tell(4)
    arrived(dx_recv.at[pl.ds(0, GROUP - 1)], 0)
    product = dx_recv[0]
    for i in range(1, GROUP):
        product = product * dx_recv[i]
    dz_send[...] = product
    for g in z_peers:
        copy(dz_send, dz_recv.at[me_g], 1, 1, at_group(g)).start()
    dz_recv[me_g] = product
    told(4)
    chunks = [(q, h) for q in range(2 * seqs) for h in range(2)]

    def run(order):
        for kind, at in order:
            if kind == "T":
                group_total(*chunks[at])
            elif kind == "L":
                local_work(at)
            elif kind == "D":
                arrived(dz_recv.at[pl.ds(0, groups - 1)], 1)
            elif kind == "S":
                group_scan(*chunks[at])
            elif kind == "M":
                member_scan(*chunks[at])
            elif kind == "F":
                finish(at)
            else:
                reduce_heads(at)

    run(ORDER)
    last = pltpu.make_async_copy(gbc_ref, gbc_out, write_sem.at[2 * seqs])
    last.start()
    sent(dx_send.at[pl.ds(0, GROUP - 1)], 0)
    sent(dz_recv.at[pl.ds(0, groups - 1)], 1)
    sent(xin_send.at[:, pl.ds(0, GROUP - 1)], X_IN)
    sent(zin_recv.at[:, pl.ds(0, groups - 1)], Z_IN)
    sent(zout_send.at[:, pl.ds(0, groups - 1)], Z_OUT)
    sent(xout_send.at[:, pl.ds(0, GROUP - 1)], X_OUT)
    sent(rs_send.at[:, pl.ds(0, peers - 1)], HEADS)
    for result in written:
        result.wait()
    last.wait()


def write_out(*refs):
    count = len(refs) // 2
    sources, results, sem = refs[:count], refs[count : 2 * count], refs[-1]
    copies = [
        pltpu.make_async_copy(a, b, sem.at[n]) for n, (a, b) in enumerate(zip(sources, results))
    ]
    for each in copies:
        each.start()
    for each in copies:
        each.wait()


def solution(mesh):
    blocks, peers = mesh.shape["seq"], mesh.shape["head"]
    groups = blocks // GROUP

    def shards(values, keys_b, queries_c, forget, skip, cotangent):
        seqs, rows, wide = values.shape
        state = keys_b.shape[-1]
        streams = 2 * seqs
        lanes, piece, part = wide // GROUP, state // groups, rows // peers
        anywhere = pl.BlockSpec(memory_space=pl.ANY)
        args = (values, keys_b, queries_c, forget, skip.reshape(1, -1), cotangent)
        results = (
            (values.shape, BF16),
            (values.shape, BF16),
            ((2, seqs, part, state), F32),
        )
        inner = pl.pallas_call(
            functools.partial(kernel, (groups, peers)),
            out_shape=tuple(pltpu.VMEM(*r) for r in results),
            in_specs=[anywhere] * len(args),
            out_specs=(anywhere,) * len(results),
            scratch_shapes=[pltpu.VMEM(a.shape, a.dtype) for a in args]
            + [pltpu.VMEM(*r) for r in results]
            + [
                pltpu.VMEM((seqs, rows, wide), F32),
                pltpu.VMEM((seqs, rows, wide), F32),
                pltpu.VMEM((seqs, rows, wide), BF16),
                pltpu.VMEM((seqs, rows, wide), BF16),
                pltpu.VMEM((seqs, rows, wide), F32),
                pltpu.VMEM((seqs, rows, wide), F32),
                pltpu.VMEM((2 * seqs, rows, state), F32),
                pltpu.VMEM((GROUP, seqs, lanes), F32),
                pltpu.VMEM((GROUP, seqs, lanes), F32),
                pltpu.VMEM((seqs, lanes), F32),
                pltpu.VMEM((groups, seqs, lanes), F32),
                pltpu.VMEM((streams, GROUP, state, lanes), F32),
                pltpu.VMEM((streams, GROUP, state, lanes), F32),
                pltpu.VMEM((streams, 2, groups // 2, piece, lanes), F32),
                pltpu.VMEM((streams, groups, piece, lanes), F32),
                pltpu.VMEM((streams, groups, piece, lanes), F32),
                pltpu.VMEM((streams, 2, groups // 2, piece, lanes), F32),
                pltpu.VMEM((streams, GROUP, state, lanes), F32),
                pltpu.VMEM((streams, GROUP, state, lanes), F32),
                pltpu.VMEM((streams, peers, part, state), F32),
                pltpu.VMEM((streams, peers, part, state), F32),
                pltpu.SemaphoreType.DMA((7,)),
                pltpu.SemaphoreType.DMA((2 + 7 * streams,)),
                pltpu.SemaphoreType.DMA((len(args),)),
                pltpu.SemaphoreType.REGULAR((5,)),
                pltpu.SemaphoreType.DMA((streams + 1,)),
            ],
            compiler_params=pltpu.CompilerParams(collective_id=0, has_side_effects=True),
        )(*args)
        return pl.pallas_call(
            write_out,
            out_shape=tuple(jax.ShapeDtypeStruct(*r) for r in results),
            in_specs=[anywhere] * len(results),
            out_specs=(anywhere,) * len(results),
            scratch_shapes=[pltpu.SemaphoreType.DMA((len(results),))],
        )(*[pltpu.with_memory_space_constraint(x, pltpu.VMEM) for x in inner])

    in_specs = (
        P(None, "seq", "head"),
        P(None, "seq", None),
        P(None, "seq", None),
        P(None, "head", "seq"),
        P("head"),
        P(None, "seq", "head"),
    )
    out_specs = (
        P(None, "seq", "head"),
        P(None, "seq", "head"),
        P(None, None, ("seq", "head"), None),
    )
    return jax.shard_map(shards, mesh=mesh, in_specs=in_specs, out_specs=out_specs, check_vma=False)
```

```python
import functools

import jax
import jax.numpy as jnp
from jax import lax
from jax.experimental import pallas as pl
from jax.experimental.pallas import tpu as pltpu
from jax.sharding import PartitionSpec as P

MESH = pl.DeviceIdType.MESH
GROUP = 4
F32 = jnp.float32
BF16 = jnp.bfloat16


def dot(a, b):
    return lax.dot_general(a, b, (((1,), (0,)), ((), ())), preferred_element_type=F32)


def dot_nt(a, b):
    return lax.dot_general(a, b, (((1,), (1,)), ((), ())), preferred_element_type=F32)


def dot_tn(a, b):
    return lax.dot_general(a, b, (((0,), (0,)), ((), ())), preferred_element_type=F32)


def iota(shape, dim):
    return lax.broadcasted_iota(jnp.int32, shape, dim)


ORDER = (
    ("T", 0), ("L", 0), ("T", 1), ("L", 1), ("T", 2), ("T", 3), ("D", 0), ("S", 0), ("T", 4), ("S", 1), ("T", 5),
    ("S", 2), ("T", 6), ("S", 3), ("T", 7), ("M", 0), ("S", 4), ("M", 1), ("S", 5), ("M", 2), ("S", 6),
    ("M", 3), ("S", 7), ("M", 4), ("F", 0), ("M", 5), ("M", 6), ("M", 7), ("F", 1), ("F", 2), ("F", 3),
    ("R", 0), ("R", 1), ("R", 2), ("R", 3),
)


def kernel(
    sizes,
    values_in, keys_in, queries_in, forget_in, skip_in, cot_in,
    mixed_out, gv_out, gbc_out,
    values_ref, keys_ref, queries_ref, forget_ref, skip_ref, cot_ref,
    mixed_ref, gv_ref, gbc_ref,
    e_head, e_tail, s_val, s_cot, mix_acc, gv_acc, bc_acc,
    dx_send, dx_recv, dz_send, dz_recv,
    xin_send, xin_recv, zin_send, zin_recv, zout_send, zout_recv, xout_send, xout_recv,
    rs_send, rs_recv,
    send_sem, recv_sem, load_sem, round_sem, write_sem,
):
    groups, peers = sizes
    seqs, rows, wide = values_ref.shape
    heads = forget_ref.shape[1]
    width = wide // heads
    state = keys_ref.shape[2]
    lanes = wide // GROUP
    half = state // 2
    piece = state // groups
    depth = groups // 2
    part = rows // peers

    me_seq = lax.axis_index("seq")
    me_head = lax.axis_index("head")
    me_x = lax.rem(me_seq, GROUP)
    me_g = me_seq // GROUP
    me_y, me_z = me_g // depth, lax.rem(me_g, depth)
    parity, me_piece = lax.rem(me_g, 2), me_g // 2

    loads = [
        pltpu.make_async_copy(src, dst, load_sem.at[n])
        for n, (src, dst) in enumerate(
            (
                (forget_in, forget_ref), (keys_in, keys_ref), (values_in, values_ref),
                (queries_in, queries_ref), (cot_in, cot_ref), (skip_in, skip_ref),
            )
        )
    ]
    for load in loads:
        load.start()

    def at_x(x):
        return (me_g * GROUP + x, me_head)

    def at_group(g):
        return (g * GROUP + me_x, me_head)

    x_peers = [lax.rem(me_x + k, GROUP) for k in (2, 1, 3)]
    away = sorted(
        ((dy, dz) for dy in range(2) for dz in range(depth) if dy or dz),
        key=lambda d: -(d[0] + min(d[1], depth - d[1])),
    )
    z_peers = [
        lax.rem(me_y + dy, 2) * depth + lax.rem(me_z + dz, depth) for dy, dz in away
    ]
    cores = 2 if peers % 2 == 0 else 1
    ring = peers // cores
    me_r, me_c = me_head // cores, lax.rem(me_head, cores)
    h_away = sorted(
        ((dr, dc) for dr in range(ring) for dc in range(cores) if dr or dc),
        key=lambda d: -min(d[0], ring - d[0]),
    )
    h_peers = [
        lax.rem(me_r + dr, ring) * cores + lax.rem(me_c + dc, cores) for dr, dc in h_away
    ]

    def steps(size, *distances):
        return sorted({d % size for d in distances} - {0})

    def z_near(*distances):
        return [
            at_group(me_y * depth + lax.rem(me_z + d, depth)) for d in steps(depth, *distances)
        ]

    y_other = [at_group((1 - me_y) * depth + me_z)]
    core_other = [(me_seq, me_r * cores + 1 - me_c)] if cores == 2 else []
    h_near = core_other + [
        (me_seq, lax.rem(me_r + d, ring) * cores + me_c) for d in steps(ring, 1, -1)
    ]
    barrier = pltpu.get_barrier_semaphore()
    near = [at_x(x) for x in x_peers] + h_near + y_other + z_near(1, -1)
    for target in near:
        pl.semaphore_signal(barrier, 1, device_id=target, device_id_type=MESH)
    rounds = (z_near(1, -1) + y_other, z_near(2, -2), y_other, h_near, core_other)

    def tell(n):
        for target in rounds[n]:
            pl.semaphore_signal(round_sem.at[n], 1, device_id=target, device_id_type=MESH)

    def told(n):
        if rounds[n]:
            pl.semaphore_wait(round_sem.at[n], len(rounds[n]))

    def copy(src, dst, send, recv, target):
        return pltpu.make_async_remote_copy(
            src_ref=src, dst_ref=dst, send_sem=send_sem.at[send], recv_sem=recv_sem.at[recv],
            device_id=target, device_id_type=MESH,
        )

    streams = 2 * seqs
    X_IN, Z_IN, Z_OUT, X_OUT, HEADS = range(2, 7)
    x_in, z_in, z_out, x_out, heads_in = (
        2, 2 + 2 * streams, 2 + 3 * streams, 2 + 5 * streams, 2 + 6 * streams
    )

    def arrived(view, slot):
        copy(view, view, slot, slot, (me_seq, me_head)).wait_recv()

    def sent(view, slot):
        copy(view, view, slot, slot, (me_seq, me_head)).wait_send()

    every = seqs * wide
    lane_head = iota((seqs * heads, every), 1) // width
    spread_heads = (lane_head == iota((seqs * heads, every), 0)).astype(BF16)
    row2, col2 = iota((2 * rows, 2 * rows), 0), iota((2 * rows, 2 * rows), 1)
    upto = jnp.where(
        row2 < rows,
        (lax.rem(col2, rows) <= row2).astype(F32),
        (lax.rem(col2, rows) > row2 - rows).astype(F32),
    ).astype(BF16)
    row_w, lane_w = iota((rows, wide), 0), lax.rem(iota((rows, wide), 1), width)

    loads[0].wait()
    flat = forget_ref[...].reshape(seqs * heads, rows)
    high = flat.astype(BF16)
    low = (flat - high.astype(F32)).astype(BF16)
    high, low = dot_tn(high, spread_heads), dot_tn(low, spread_heads)
    sums = dot(upto, jnp.concatenate([high, low], axis=0).astype(BF16))
    for s in range(seqs):
        cols = slice(s * wide, (s + 1) * wide)
        e_head[s] = jnp.exp(-sums[:rows, cols])
        e_tail[s] = jnp.exp(-sums[rows:, cols])
        total = jnp.exp(-sums[rows - 1 : rows, cols])
        for j in range(GROUP):
            dx_send[j, s : s + 1] = total[:, j * lanes : (j + 1) * lanes]
    dx_recv[me_x] = dx_send[me_x]

    def local_state(q):
        s, back = q // 2, q % 2
        if back:
            scaled = (cot_ref[s].astype(F32) * e_head[s]).astype(BF16)
            s_cot[s] = scaled
            local = dot_tn(queries_ref[s], scaled)
        else:
            scaled = (values_ref[s].astype(F32) * e_tail[s]).astype(BF16)
            s_val[s] = scaled
            local = dot_tn(keys_ref[s], scaled)
        for j in range(GROUP):
            xin_send[q, j] = local[:, j * lanes : (j + 1) * lanes]

    def half_rows(h):
        return pl.ds(h * half, half)

    def send_state(q):
        for h in range(2):
            for x in x_peers:
                copy(
                    xin_send.at[q, x, half_rows(h)], xin_recv.at[q, me_x, half_rows(h)],
                    X_IN, x_in + 2 * q + h, at_x(x),
                ).start()
        xin_recv[q, me_x] = xin_send[q, me_x]

    loads[1].wait()
    loads[2].wait()
    local_state(0)
    pl.semaphore_wait(barrier, len(near))
    tell(0)
    tell(3)
    for x in x_peers:
        copy(dx_send.at[x], dx_recv.at[me_x], 0, 0, at_x(x)).start()
    send_state(0)
    for load in loads[3:]:
        load.wait()
    for q in range(1, 2 * seqs):
        local_state(q)
        send_state(q)

    def local_work(s):
        mine = slice(s * wide, (s + 1) * wide)
        zero = jnp.zeros((rows, wide), F32)

        def gap(keep, span):
            picked = jnp.concatenate(
                [jnp.where(keep, high[:, mine], zero), jnp.where(keep, low[:, mine], zero)], axis=0
            ).astype(BF16)
            return jnp.exp(-dot(span, picked))

        decay = jnp.where(lane_w <= row_w, gap(row_w > lane_w, upto[:rows]), 0.0)
        decay_t = jnp.where(lane_w >= row_w, gap(row_w <= lane_w, upto[rows:]), 0.0)
        keys, queries = keys_ref[s], queries_ref[s]
        keys2 = jnp.concatenate([keys, keys], axis=0)
        queries2 = jnp.concatenate([queries, queries], axis=0)
        copies = wide // (2 * rows)
        scores = jnp.concatenate([dot_nt(queries, keys2)] * copies, axis=1)
        scores_t = jnp.concatenate([dot_nt(keys, queries2)] * copies, axis=1)
        weights = (scores * decay).astype(BF16)
        weights_t = (scores_t * decay_t).astype(BF16)
        quad = 4 * width
        mask = (iota((quad, quad), 0) // rows == iota((quad, quad), 1) // width).astype(BF16)
        grad_sum = None
        for c in range(wide // quad):
            cols = slice(c * quad, (c + 1) * quad)
            val, cot = values_ref[s, :, cols], cot_ref[s, :, cols]
            val_diag = jnp.concatenate([val] * 4, axis=0) * mask
            cot_diag = jnp.concatenate([cot] * 4, axis=0) * mask
            skip_row = jnp.concatenate(
                [
                    jnp.broadcast_to(skip_ref[0:1, 4 * c + i : 4 * c + i + 1], (1, width))
                    for i in range(4)
                ],
                axis=1,
            )
            mix_acc[s, :, cols] = dot(weights[:, cols], val_diag) + skip_row * val.astype(F32)
            gv_acc[s, :, cols] = dot(weights_t[:, cols], cot_diag) + skip_row * cot.astype(F32)
            grad_w = dot_nt(cot, val_diag) * decay[:, cols]
            for i in range(2):
                term = grad_w[:, i * 2 * width : (i + 1) * 2 * width]
                grad_sum = term if grad_sum is None else grad_sum + term
        grad_sum = grad_sum.astype(BF16)
        bc_acc[2 * s] = dot(grad_sum, keys2)
        folded = dot_tn(grad_sum, queries)
        bc_acc[2 * s + 1] = folded[:rows] + folded[rows:]

    def decay_x(s, i):
        return dx_recv[i, s : s + 1]

    def decay_z(s, g):
        return dz_recv[g, s : s + 1]

    def group_total(q, h):
        s, back = q // 2, q % 2
        arrived(xin_recv.at[q, pl.ds(0, GROUP - 1), half_rows(h)], x_in + 2 * q + h)
        order = range(GROUP - 1, -1, -1) if back else range(GROUP)
        total = None
        for i in order:
            term = xin_recv[q, i, half_rows(h)]
            total = term if total is None else decay_x(s, i) * total + term
        zin_send[q, h] = total.reshape(depth, piece, lanes)
        first = lax.rem(me_z + h, 2)

        def send(dy, k):
            g = lax.rem(me_y + dy, 2) * depth + lax.rem(me_z + first + 2 * k, depth)
            copy(
                zin_send.at[q, h, g // 2], zin_recv.at[q, me_g],
                Z_IN, z_in + q, at_group(g),
            ).start()

        hops = sorted(range(depth // 2), key=lambda k: -min(2 * k + 1, depth - 2 * k))
        for dy, k in [(1, k) for k in hops] + [(0, k) for k in hops if k]:
            send(dy, k)

        @pl.when(parity != h)
        def _():
            send(0, 0)

        @pl.when(parity == h)
        def _():
            zin_recv[q, me_g] = zin_send[q, h, me_piece]

    def group_scan(q, h):
        s, back = q // 2, q % 2

        @pl.when(parity == h)
        def _():
            arrived(zin_recv.at[q, pl.ds(0, groups - 1)], z_in + q)
            order = range(groups - 1, -1, -1) if back else range(groups)
            carry = jnp.zeros((piece, lanes), F32)
            for n, g in enumerate(order):
                zout_send[q, g] = carry
                if n < groups - 1:
                    carry = decay_z(s, g) * carry + zin_recv[q, g]
            for g in z_peers:
                copy(
                    zout_send.at[q, g], zout_recv.at[q, h, me_piece],
                    Z_OUT, z_out + 2 * q + h, at_group(g),
                ).start()
            zout_recv[q, h, me_piece] = zout_send[q, me_g]

    def member_scan(q, h):
        s, back = q // 2, q % 2

        @pl.when(parity != h)
        def _():
            arrived(zout_recv.at[q, h], z_out + 2 * q + h)

        @pl.when(parity == h)
        def _():
            arrived(zout_recv.at[q, h, pl.ds(0, depth - 1)], z_out + 2 * q + h)

        order = range(GROUP - 1, -1, -1) if back else range(GROUP)
        carry = zout_recv[q, h].reshape(half, lanes)
        for n, i in enumerate(order):
            xout_send[q, i, half_rows(h)] = carry
            if n < GROUP - 1:
                carry = decay_x(s, i) * carry + xin_recv[q, i, half_rows(h)]
        for x in x_peers:
            copy(
                xout_send.at[q, x, half_rows(h)], xout_recv.at[q, me_x, half_rows(h)],
                X_OUT, x_out + q, at_x(x),
            ).start()
        xout_recv[q, me_x, half_rows(h)] = xout_send[q, me_x, half_rows(h)]

    written = []

    def finish(q):
        s, back = q // 2, q % 2
        arrived(xout_recv.at[q, pl.ds(0, GROUP - 1)], x_out + q)
        carried = jnp.concatenate([xout_recv[q, j] for j in range(GROUP)], axis=1).astype(BF16)
        if back:
            grad = bc_acc[2 * s + 1] + dot_nt(s_val[s], carried)
        else:
            grad = bc_acc[2 * s] + dot_nt(s_cot[s], carried)
        rs_send[q] = grad.reshape(peers, part, state)
        for p in h_peers:
            copy(
                rs_send.at[q, p], rs_recv.at[q, me_head], HEADS, heads_in + q, (me_seq, p)
            ).start()
        rs_recv[q, me_head] = rs_send[q, me_head]
        if back:
            gv_ref[s] = (gv_acc[s] + e_tail[s] * dot(keys_ref[s], carried)).astype(BF16)
        else:
            mixed_ref[s] = (mix_acc[s] + e_head[s] * dot(queries_ref[s], carried)).astype(BF16)
        source, result = (gv_ref, gv_out) if back else (mixed_ref, mixed_out)
        written.append(pltpu.make_async_copy(source.at[s], result.at[s], write_sem.at[q]))
        written[-1].start()

    def reduce_heads(q):
        s, back = q // 2, q % 2
        arrived(rs_recv.at[q, pl.ds(0, peers - 1)], heads_in + q)
        total = rs_recv[q, 0]
        for h in range(1, peers):
            total = total + rs_recv[q, h]
        gbc_ref[1 - back, s] = total

    told(0)
    tell(1)
    arrived(dx_recv.at[pl.ds(0, GROUP - 1)], 0)
    product = dx_recv[0]
    for i in range(1, GROUP):
        product = product * dx_recv[i]
    dz_send[...] = product
    told(1)
    tell(2)
    told(3)
    tell(4)
    told(2)
    for g in z_peers:
        copy(dz_send, dz_recv.at[me_g], 1, 1, at_group(g)).start()
    dz_recv[me_g] = product
    told(4)
    chunks = [(q, h) for q in range(2 * seqs) for h in range(2)]

    def run(order):
        for kind, at in order:
            if kind == "T":
                group_total(*chunks[at])
            elif kind == "L":
                local_work(at)
            elif kind == "D":
                arrived(dz_recv.at[pl.ds(0, groups - 1)], 1)
            elif kind == "S":
                group_scan(*chunks[at])
            elif kind == "M":
                member_scan(*chunks[at])
            elif kind == "F":
                finish(at)
            else:
                reduce_heads(at)

    run(ORDER)
    last = pltpu.make_async_copy(gbc_ref, gbc_out, write_sem.at[2 * seqs])
    last.start()
    sent(dx_send.at[pl.ds(0, GROUP - 1)], 0)
    sent(dz_recv.at[pl.ds(0, groups - 1)], 1)
    sent(xin_send.at[:, pl.ds(0, GROUP - 1)], X_IN)
    sent(zin_recv.at[:, pl.ds(0, groups - 1)], Z_IN)
    sent(zout_send.at[:, pl.ds(0, groups - 1)], Z_OUT)
    sent(xout_send.at[:, pl.ds(0, GROUP - 1)], X_OUT)
    sent(rs_send.at[:, pl.ds(0, peers - 1)], HEADS)
    for result in written:
        result.wait()
    last.wait()


def write_out(*refs):
    count = len(refs) // 2
    sources, results, sem = refs[:count], refs[count : 2 * count], refs[-1]
    copies = [
        pltpu.make_async_copy(a, b, sem.at[n]) for n, (a, b) in enumerate(zip(sources, results))
    ]
    for each in copies:
        each.start()
    for each in copies:
        each.wait()


def solution(mesh):
    blocks, peers = mesh.shape["seq"], mesh.shape["head"]
    groups = blocks // GROUP

    def shards(values, keys_b, queries_c, forget, skip, cotangent):
        seqs, rows, wide = values.shape
        state = keys_b.shape[-1]
        streams = 2 * seqs
        lanes, piece, part = wide // GROUP, state // groups, rows // peers
        anywhere = pl.BlockSpec(memory_space=pl.ANY)
        args = (values, keys_b, queries_c, forget, skip.reshape(1, -1), cotangent)
        results = (
            (values.shape, BF16),
            (values.shape, BF16),
            ((2, seqs, part, state), F32),
        )
        inner = pl.pallas_call(
            functools.partial(kernel, (groups, peers)),
            out_shape=tuple(pltpu.VMEM(*r) for r in results),
            in_specs=[anywhere] * len(args),
            out_specs=(anywhere,) * len(results),
            scratch_shapes=[pltpu.VMEM(a.shape, a.dtype) for a in args]
            + [pltpu.VMEM(*r) for r in results]
            + [
                pltpu.VMEM((seqs, rows, wide), F32),
                pltpu.VMEM((seqs, rows, wide), F32),
                pltpu.VMEM((seqs, rows, wide), BF16),
                pltpu.VMEM((seqs, rows, wide), BF16),
                pltpu.VMEM((seqs, rows, wide), F32),
                pltpu.VMEM((seqs, rows, wide), F32),
                pltpu.VMEM((2 * seqs, rows, state), F32),
                pltpu.VMEM((GROUP, seqs, lanes), F32),
                pltpu.VMEM((GROUP, seqs, lanes), F32),
                pltpu.VMEM((seqs, lanes), F32),
                pltpu.VMEM((groups, seqs, lanes), F32),
                pltpu.VMEM((streams, GROUP, state, lanes), F32),
                pltpu.VMEM((streams, GROUP, state, lanes), F32),
                pltpu.VMEM((streams, 2, groups // 2, piece, lanes), F32),
                pltpu.VMEM((streams, groups, piece, lanes), F32),
                pltpu.VMEM((streams, groups, piece, lanes), F32),
                pltpu.VMEM((streams, 2, groups // 2, piece, lanes), F32),
                pltpu.VMEM((streams, GROUP, state, lanes), F32),
                pltpu.VMEM((streams, GROUP, state, lanes), F32),
                pltpu.VMEM((streams, peers, part, state), F32),
                pltpu.VMEM((streams, peers, part, state), F32),
                pltpu.SemaphoreType.DMA((7,)),
                pltpu.SemaphoreType.DMA((2 + 7 * streams,)),
                pltpu.SemaphoreType.DMA((len(args),)),
                pltpu.SemaphoreType.REGULAR((5,)),
                pltpu.SemaphoreType.DMA((streams + 1,)),
            ],
            compiler_params=pltpu.CompilerParams(collective_id=0, has_side_effects=True),
        )(*args)
        return pl.pallas_call(
            write_out,
            out_shape=tuple(jax.ShapeDtypeStruct(*r) for r in results),
            in_specs=[anywhere] * len(results),
            out_specs=(anywhere,) * len(results),
            scratch_shapes=[pltpu.SemaphoreType.DMA((len(results),))],
        )(*[pltpu.with_memory_space_constraint(x, pltpu.VMEM) for x in inner])

    in_specs = (
        P(None, "seq", "head"),
        P(None, "seq", None),
        P(None, "seq", None),
        P(None, "head", "seq"),
        P("head"),
        P(None, "seq", "head"),
    )
    out_specs = (
        P(None, "seq", "head"),
        P(None, "seq", "head"),
        P(None, None, ("seq", "head"), None),
    )
    return jax.shard_map(shards, mesh=mesh, in_specs=in_specs, out_specs=out_specs, check_vma=False)
```

```python
import functools

import jax
import jax.numpy as jnp
from jax import lax
from jax.experimental import pallas as pl
from jax.experimental.pallas import tpu as pltpu
from jax.sharding import PartitionSpec as P

MESH = pl.DeviceIdType.MESH
GROUP = 4
F32 = jnp.float32
BF16 = jnp.bfloat16


def dot(a, b):
    return lax.dot_general(a, b, (((1,), (0,)), ((), ())), preferred_element_type=F32)


def dot_nt(a, b):
    return lax.dot_general(a, b, (((1,), (1,)), ((), ())), preferred_element_type=F32)


def dot_tn(a, b):
    return lax.dot_general(a, b, (((0,), (0,)), ((), ())), preferred_element_type=F32)


def iota(shape, dim):
    return lax.broadcasted_iota(jnp.int32, shape, dim)


ORDER = (
    ("K", 0), ("I", 1), ("B", 0), ("I", 2), ("K", 1), ("T", 0), ("B", 1), ("I", 3), ("L", 0), ("T", 1),
    ("B", 2), ("L", 1), ("T", 2), ("B", 3), ("D", 0), ("S", 0), ("T", 3), ("S", 1), ("S", 2), ("S", 3),
    ("K", 2), ("M", 0), ("M", 1), ("C", 0), ("M", 2), ("C", 1), ("M", 3), ("C", 2), ("C", 3), ("F", 0),
    ("Z", 0), ("F", 1), ("Z", 1), ("Z", 2), ("F", 2), ("F", 3), ("Z", 3),
)


def kernel(
    sizes,
    values_in, keys_in, queries_in, forget_in, skip_in, cot_in,
    mixed_out, gv_out, gbc_out,
    values_ref, keys_ref, queries_ref, forget_ref, skip_ref, cot_ref,
    mixed_ref, gv_ref, gbc_ref,
    e_head, e_tail, mix_acc, gv_acc, bc_acc,
    dx_send, dx_recv, dz_send, dz_recv,
    map_send, maps, slice_send, slices, states,
    zin_send, zin_recv, zout_send, zout_recv, cross_send, cross,
    grads, pair_recv, sums_send, sums_recv,
    send_sem, recv_sem, load_sem, round_sem, write_sem,
):
    groups, peers = sizes
    seqs, rows, wide = values_ref.shape
    heads = forget_ref.shape[1]
    width = wide // heads
    state = keys_ref.shape[2]
    lanes = wide // GROUP
    piece = state // groups
    depth = groups // 2
    part = rows // peers

    me_seq = lax.axis_index("seq")
    me_head = lax.axis_index("head")
    me_x = lax.rem(me_seq, GROUP)
    me_g = me_seq // GROUP
    me_y, me_z = me_g // depth, lax.rem(me_g, depth)

    loads = [
        pltpu.make_async_copy(src, dst, load_sem.at[n])
        for n, (src, dst) in enumerate(
            (
                (forget_in, forget_ref), (keys_in, keys_ref), (values_in, values_ref),
                (queries_in, queries_ref), (cot_in, cot_ref), (skip_in, skip_ref),
            )
        )
    ]
    for load in loads:
        load.start()

    def at_x(x):
        return (me_g * GROUP + x, me_head)

    def at_group(g):
        return (g * GROUP + me_x, me_head)

    x_peers = [lax.rem(me_x + k, GROUP) for k in (2, 1, 3)]
    away = sorted(
        ((dy, dz) for dy in range(2) for dz in range(depth) if dy or dz),
        key=lambda d: -(d[0] + min(d[1], depth - d[1])),
    )
    z_peers = [
        lax.rem(me_y + dy, 2) * depth + lax.rem(me_z + dz, depth) for dy, dz in away
    ]
    cores = 2
    ring = peers // cores
    share = rows // cores
    me_r, me_c = me_head // cores, lax.rem(me_head, cores)
    far = sorted(
        ((dr, dx) for dr in range(ring) for dx in range(GROUP) if dr or dx),
        key=lambda d: -(2 * min(d[0], ring - d[0]) + min(d[1], GROUP - d[1])),
    )
    members = [(lax.rem(me_r + dr, ring), lax.rem(me_x + dx, GROUP)) for dr, dx in far]

    def at_member(r, x):
        return (me_g * GROUP + x, r * cores + me_c)

    def at_ring(r):
        return (me_seq, r * cores + me_c)

    def steps(size, *distances):
        return sorted({d % size for d in distances} - {0})

    def z_near(*distances):
        return [
            at_group(me_y * depth + lax.rem(me_z + d, depth)) for d in steps(depth, *distances)
        ]

    y_other = [at_group((1 - me_y) * depth + me_z)]
    core_other = (me_seq, me_r * cores + 1 - me_c)
    r_near = [at_ring(lax.rem(me_r + d, ring)) for d in steps(ring, 1, -1)]
    barrier = pltpu.get_barrier_semaphore()
    near = [at_x(x) for x in x_peers] + [core_other] + r_near + y_other + z_near(1, -1, 2, -2)
    for target in near:
        pl.semaphore_signal(barrier, 1, device_id=target, device_id_type=MESH)
    r_far = [at_ring(lax.rem(me_r + 2, ring))] if ring > 3 else []
    rounds = (z_near(2, -2) + y_other, y_other, r_near, r_far)

    def tell(n):
        for target in rounds[n]:
            pl.semaphore_signal(round_sem.at[n], 1, device_id=target, device_id_type=MESH)

    def told(n):
        if rounds[n]:
            pl.semaphore_wait(round_sem.at[n], len(rounds[n]))

    def copy(src, dst, send, recv, target):
        return pltpu.make_async_remote_copy(
            src_ref=src, dst_ref=dst, send_sem=send_sem.at[send], recv_sem=recv_sem.at[recv],
            device_id=target, device_id_type=MESH,
        )

    streams = 2 * seqs
    MAPS, PASSED, SLICES, Z_IN, Z_OUT, CROSS, PAIR, SUMS = range(2, 10)

    def slot(phase, q):
        return 2 + (phase - 2) * streams + q

    def arrived(view, at):
        copy(view, view, at, at, (me_seq, me_head)).wait_recv()

    def sent(view, at):
        copy(view, view, at, at, (me_seq, me_head)).wait_send()

    every = seqs * wide
    lane_head = iota((seqs * heads, every), 1) // width
    spread_heads = (lane_head == iota((seqs * heads, every), 0)).astype(BF16)
    row2, col2 = iota((2 * rows, 2 * rows), 0), iota((2 * rows, 2 * rows), 1)
    upto = jnp.where(
        row2 < rows,
        (lax.rem(col2, rows) <= row2).astype(F32),
        (lax.rem(col2, rows) > row2 - rows).astype(F32),
    ).astype(BF16)
    row_w, lane_w = iota((rows, wide), 0), lax.rem(iota((rows, wide), 1), width)

    loads[0].wait()
    flat = forget_ref[...].reshape(seqs * heads, rows)
    high = flat.astype(BF16)
    low = (flat - high.astype(F32)).astype(BF16)
    high, low = dot_tn(high, spread_heads), dot_tn(low, spread_heads)
    sums = dot(upto, jnp.concatenate([high, low], axis=0).astype(BF16))
    for s in range(seqs):
        cols = slice(s * wide, (s + 1) * wide)
        e_head[s] = jnp.exp(-sums[:rows, cols])
        e_tail[s] = jnp.exp(-sums[rows:, cols])
        total = jnp.exp(-sums[rows - 1 : rows, cols])
        for j in range(GROUP):
            dx_send[j, s : s + 1] = total[:, j * lanes : (j + 1) * lanes]
    dx_recv[me_x] = dx_send[me_x]

    mine = pl.ds(pl.multiple_of(me_c * share, share), share)

    def send_inputs(q):
        s, back = q // 2, q % 2
        map_ref, input_ref, scale = (
            (queries_ref, cot_ref, e_head) if back else (keys_ref, values_ref, e_tail)
        )
        map_send[q] = map_ref[s].astype(F32)
        scaled = input_ref[s].astype(F32) * scale[s]
        for j in range(GROUP):
            slice_send[q, j] = scaled[:, j * lanes : (j + 1) * lanes]
        if q == 0:
            pl.semaphore_wait(barrier, len(near))
            tell(0)
            tell(2)
            for x in x_peers:
                copy(dx_send.at[x], dx_recv.at[me_x], 0, 0, at_x(x)).start()
        for x in x_peers:
            copy(
                map_send.at[q, mine], maps.at[q, me_x, mine], MAPS, slot(MAPS, q), at_x(x)
            ).start()
        for x in x_peers:
            copy(
                slice_send.at[q, x], slices.at[q, me_x], SLICES, slot(SLICES, q), at_x(x)
            ).start()
        maps[q, me_x, mine] = map_send[q, mine]
        slices[q, me_x] = slice_send[q, me_x]

    loads[1].wait()
    loads[2].wait()
    send_inputs(0)
    for load in loads[3:]:
        load.wait()

    def local_work(s):
        own = slice(s * wide, (s + 1) * wide)
        zero = jnp.zeros((rows, wide), F32)

        def gap(keep, span):
            picked = jnp.concatenate(
                [jnp.where(keep, high[:, own], zero), jnp.where(keep, low[:, own], zero)], axis=0
            ).astype(BF16)
            return jnp.exp(-dot(span, picked))

        decay = jnp.where(lane_w <= row_w, gap(row_w > lane_w, upto[:rows]), 0.0)
        decay_t = jnp.where(lane_w >= row_w, gap(row_w <= lane_w, upto[rows:]), 0.0)
        keys, queries = keys_ref[s], queries_ref[s]
        keys2 = jnp.concatenate([keys, keys], axis=0)
        queries2 = jnp.concatenate([queries, queries], axis=0)
        copies = wide // (2 * rows)
        scores = jnp.concatenate([dot_nt(queries, keys2)] * copies, axis=1)
        scores_t = jnp.concatenate([dot_nt(keys, queries2)] * copies, axis=1)
        weights = (scores * decay).astype(BF16)
        weights_t = (scores_t * decay_t).astype(BF16)
        quad = 4 * width
        mask = (iota((quad, quad), 0) // rows == iota((quad, quad), 1) // width).astype(BF16)
        grad_sum = None
        for c in range(wide // quad):
            cols = slice(c * quad, (c + 1) * quad)
            val, cot = values_ref[s, :, cols], cot_ref[s, :, cols]
            val_diag = jnp.concatenate([val] * 4, axis=0) * mask
            cot_diag = jnp.concatenate([cot] * 4, axis=0) * mask
            skip_row = jnp.concatenate(
                [
                    jnp.broadcast_to(skip_ref[0:1, 4 * c + i : 4 * c + i + 1], (1, width))
                    for i in range(4)
                ],
                axis=1,
            )
            mix_acc[s, :, cols] = dot(weights[:, cols], val_diag) + skip_row * val.astype(F32)
            gv_acc[s, :, cols] = dot(weights_t[:, cols], cot_diag) + skip_row * cot.astype(F32)
            grad_w = dot_nt(cot, val_diag) * decay[:, cols]
            for i in range(2):
                term = grad_w[:, i * 2 * width : (i + 1) * 2 * width]
                grad_sum = term if grad_sum is None else grad_sum + term
        grad_sum = grad_sum.astype(BF16)
        bc_acc[2 * s] = dot(grad_sum, keys2)
        folded = dot_tn(grad_sum, queries)
        bc_acc[2 * s + 1] = folded[:rows] + folded[rows:]

    def decay_x(s, i):
        return dx_recv[i, s : s + 1]

    def decay_z(s, g):
        return dz_recv[g, s : s + 1]

    def pass_maps(q):
        arrived(maps.at[q, pl.ds(0, GROUP - 1), pl.ds(0, share)], slot(MAPS, q))
        view = maps.at[q, pl.ds(0, GROUP), mine]
        copy(view, view, PASSED, slot(PASSED, q), core_other).start()

    def group_total(q):
        s, back = q // 2, q % 2
        arrived(slices.at[q, pl.ds(0, GROUP - 1)], slot(SLICES, q))
        arrived(maps.at[q, pl.ds(0, GROUP), pl.ds(0, share)], slot(PASSED, q))
        weighted, weight = [None] * GROUP, None
        for i in range(GROUP) if back else range(GROUP - 1, -1, -1):
            weighted[i] = slices[q, i] if weight is None else weight * slices[q, i]
            weight = decay_x(s, i) if weight is None else weight * decay_x(s, i)
        all_maps = maps[q].reshape(GROUP * rows, state).astype(BF16)
        total = dot_tn(all_maps, jnp.concatenate(weighted, axis=0).astype(BF16))
        zin_send[q] = total.reshape(groups, piece, lanes)
        for g in z_peers:
            copy(
                zin_send.at[q, g], zin_recv.at[q, me_g], Z_IN, slot(Z_IN, q), at_group(g)
            ).start()
        zin_recv[q, me_g] = zin_send[q, me_g]
        for i in range(1, GROUP) if back else range(GROUP - 1):
            states[q, i] = dot_tn(maps[q, i].astype(BF16), slices[q, i].astype(BF16))

    def group_scan(q):
        s, back = q // 2, q % 2
        arrived(zin_recv.at[q, pl.ds(0, groups - 1)], slot(Z_IN, q))
        order = range(groups - 1, -1, -1) if back else range(groups)
        carry = jnp.zeros((piece, lanes), F32)
        for n, g in enumerate(order):
            zout_send[q, g] = carry
            if n < groups - 1:
                carry = decay_z(s, g) * carry + zin_recv[q, g]
        for g in z_peers:
            copy(
                zout_send.at[q, g], zout_recv.at[q, me_g], Z_OUT, slot(Z_OUT, q), at_group(g)
            ).start()
        zout_recv[q, me_g] = zout_send[q, me_g]

    def member_scan(q):
        s, back = q // 2, q % 2
        other = q - 1 if back else q + 1
        arrived(zout_recv.at[q, pl.ds(0, groups - 1)], slot(Z_OUT, q))
        order = range(GROUP - 1, -1, -1) if back else range(GROUP)
        carry = zout_recv[q].reshape(state, lanes)
        carried = [None] * GROUP
        for n, i in enumerate(order):
            carried[i] = carry.astype(BF16)
            grad = dot_nt(slices[other, i].astype(BF16), carried[i])
            grad = grad.reshape(ring, cores, part, state)
            for c in range(cores):
                grads[q, c, :, i] = grad[:, c]
            if n < GROUP - 1:
                carry = decay_x(s, i) * carry + states[q, i]
        own = bc_acc[2 * s + back].reshape(ring, cores, part, state)
        for c in range(cores):
            grads[q, c, :, me_x] = grads[q, c, :, me_x] + own[:, c]
        copy(grads.at[q, 1 - me_c], pair_recv.at[q], PAIR, slot(PAIR, q), core_other).start()
        for i in order:
            cross_send[q, i] = dot(maps[other, i].astype(BF16), carried[i])
        for x in x_peers:
            copy(
                cross_send.at[q, x], cross.at[q, me_x], CROSS, slot(CROSS, q), at_x(x)
            ).start()
        cross[q, me_x] = cross_send[q, me_x]

    def sum_pair(q):
        arrived(pair_recv.at[q], slot(PAIR, q))
        sums_send[q] = grads[q, me_c] + pair_recv[q]
        me = me_r * GROUP + me_x
        for r, x in members:
            copy(
                sums_send.at[q, r, x], sums_recv.at[q, me], SUMS, slot(SUMS, q), at_member(r, x)
            ).start()
        sums_recv[q, me] = sums_send[q, me_r, me_x]

    def sum_all(q):
        s, back = q // 2, q % 2
        arrived(sums_recv.at[q, pl.ds(0, len(members))], slot(SUMS, q))
        total = sums_recv[q, 0]
        for n in range(1, ring * GROUP):
            total = total + sums_recv[q, n]
        gbc_ref[1 - back, s] = total

    written = []

    def finish(q):
        s, back = q // 2, q % 2
        arrived(cross.at[q, pl.ds(0, GROUP - 1)], slot(CROSS, q))
        terms = jnp.concatenate([cross[q, j] for j in range(GROUP)], axis=1)
        if back:
            gv_ref[s] = (gv_acc[s] + e_tail[s] * terms).astype(BF16)
        else:
            mixed_ref[s] = (mix_acc[s] + e_head[s] * terms).astype(BF16)
        source, result = (gv_ref, gv_out) if back else (mixed_ref, mixed_out)
        written.append(pltpu.make_async_copy(source.at[s], result.at[s], write_sem.at[q]))
        written[-1].start()

    def hear_near():
        told(0)
        tell(1)
        told(2)
        tell(3)

    def group_decays():
        arrived(dx_recv.at[pl.ds(0, GROUP - 1)], 0)
        product = dx_recv[0]
        for i in range(1, GROUP):
            product = product * dx_recv[i]
        dz_send[...] = product
        dz_recv[me_g] = product
        told(1)
        for g in z_peers:
            copy(dz_send, dz_recv.at[me_g], 1, 1, at_group(g)).start()

    def all_decays():
        arrived(dz_recv.at[pl.ds(0, groups - 1)], 1)

    work = {
        "I": send_inputs, "B": pass_maps, "T": group_total, "S": group_scan, "M": member_scan, "C": sum_pair,
        "Z": sum_all, "F": finish, "L": local_work,
        "K": lambda n: (hear_near, group_decays, lambda: told(3))[n](), "D": lambda _: all_decays(),
    }

    def run(order):
        for kind, at in order:
            work[kind](at)

    run(ORDER)
    last = pltpu.make_async_copy(gbc_ref, gbc_out, write_sem.at[2 * seqs])
    last.start()
    sent(dx_send.at[pl.ds(0, GROUP - 1)], 0)
    sent(dz_recv.at[pl.ds(0, groups - 1)], 1)
    sent(maps.at[:, pl.ds(0, GROUP - 1), pl.ds(0, share)], MAPS)
    sent(maps.at[:, :, pl.ds(0, share)], PASSED)
    sent(slices.at[:, pl.ds(0, GROUP - 1)], SLICES)
    sent(zin_recv.at[:, pl.ds(0, groups - 1)], Z_IN)
    sent(zout_recv.at[:, pl.ds(0, groups - 1)], Z_OUT)
    sent(cross.at[:, pl.ds(0, GROUP - 1)], CROSS)
    sent(pair_recv, PAIR)
    sent(sums_recv.at[:, pl.ds(0, len(members))], SUMS)
    for result in written:
        result.wait()
    last.wait()


def write_out(*refs):
    count = len(refs) // 2
    sources, results, sem = refs[:count], refs[count : 2 * count], refs[-1]
    copies = [
        pltpu.make_async_copy(a, b, sem.at[n]) for n, (a, b) in enumerate(zip(sources, results))
    ]
    for each in copies:
        each.start()
    for each in copies:
        each.wait()


def solution(mesh):
    blocks, peers = mesh.shape["seq"], mesh.shape["head"]
    groups = blocks // GROUP

    def shards(values, keys_b, queries_c, forget, skip, cotangent):
        seqs, rows, wide = values.shape
        state = keys_b.shape[-1]
        streams = 2 * seqs
        lanes, piece, part = wide // GROUP, state // groups, rows // peers
        anywhere = pl.BlockSpec(memory_space=pl.ANY)
        args = (values, keys_b, queries_c, forget, skip.reshape(1, -1), cotangent)
        results = (
            (values.shape, BF16),
            (values.shape, BF16),
            ((2, seqs, part, state), F32),
        )
        inner = pl.pallas_call(
            functools.partial(kernel, (groups, peers)),
            out_shape=tuple(pltpu.VMEM(*r) for r in results),
            in_specs=[anywhere] * len(args),
            out_specs=(anywhere,) * len(results),
            scratch_shapes=[pltpu.VMEM(a.shape, a.dtype) for a in args]
            + [pltpu.VMEM(*r) for r in results]
            + [
                *[pltpu.VMEM((seqs, rows, wide), F32)] * 4,
                pltpu.VMEM((2 * seqs, rows, state), F32),
                *[pltpu.VMEM((GROUP, seqs, lanes), F32)] * 2,
                pltpu.VMEM((seqs, lanes), F32),
                pltpu.VMEM((groups, seqs, lanes), F32),
                pltpu.VMEM((streams, rows, state), F32),
                pltpu.VMEM((streams, GROUP, rows, state), F32),
                *[pltpu.VMEM((streams, GROUP, rows, lanes), F32)] * 2,
                pltpu.VMEM((streams, GROUP, state, lanes), F32),
                *[pltpu.VMEM((streams, groups, piece, lanes), F32)] * 4,
                *[pltpu.VMEM((streams, GROUP, rows, lanes), F32)] * 2,
                pltpu.VMEM((streams, 2, peers // 2, GROUP, part, state), F32),
                *[pltpu.VMEM((streams, peers // 2, GROUP, part, state), F32)] * 2,
                pltpu.VMEM((streams, peers // 2 * GROUP, part, state), F32),
                pltpu.SemaphoreType.DMA((10,)),
                pltpu.SemaphoreType.DMA((2 + 8 * streams,)),
                pltpu.SemaphoreType.DMA((len(args),)),
                pltpu.SemaphoreType.REGULAR((4,)),
                pltpu.SemaphoreType.DMA((streams + 1,)),
            ],
            compiler_params=pltpu.CompilerParams(collective_id=0, has_side_effects=True),
        )(*args)
        return pl.pallas_call(
            write_out,
            out_shape=tuple(jax.ShapeDtypeStruct(*r) for r in results),
            in_specs=[anywhere] * len(results),
            out_specs=(anywhere,) * len(results),
            scratch_shapes=[pltpu.SemaphoreType.DMA((len(results),))],
        )(*[pltpu.with_memory_space_constraint(x, pltpu.VMEM) for x in inner])

    in_specs = (
        P(None, "seq", "head"),
        P(None, "seq", None),
        P(None, "seq", None),
        P(None, "head", "seq"),
        P("head"),
        P(None, "seq", "head"),
    )
    out_specs = (
        P(None, "seq", "head"),
        P(None, "seq", "head"),
        P(None, None, ("seq", "head"), None),
    )
    return jax.shard_map(shards, mesh=mesh, in_specs=in_specs, out_specs=out_specs, check_vma=False)
```

```python
import functools

import jax
import jax.numpy as jnp
from jax import lax
from jax.experimental import pallas as pl
from jax.experimental.pallas import tpu as pltpu
from jax.sharding import PartitionSpec as P

MESH = pl.DeviceIdType.MESH
GROUP = 4
F32 = jnp.float32
BF16 = jnp.bfloat16


def dot(a, b):
    return lax.dot_general(a, b, (((1,), (0,)), ((), ())), preferred_element_type=F32)


def dot_nt(a, b):
    return lax.dot_general(a, b, (((1,), (1,)), ((), ())), preferred_element_type=F32)


def dot_tn(a, b):
    return lax.dot_general(a, b, (((0,), (0,)), ((), ())), preferred_element_type=F32)


def iota(shape, dim):
    return lax.broadcasted_iota(jnp.int32, shape, dim)


ORDER = (
    ("K", 0), ("I", 1), ("B", 0), ("I", 2), ("K", 1), ("T", 0), ("B", 1), ("I", 3), ("L", 0), ("T", 1),
    ("B", 2), ("L", 1), ("T", 2), ("B", 3), ("D", 0), ("S", 0), ("T", 3), ("S", 1), ("S", 2), ("S", 3),
    ("K", 2), ("M", 0), ("Y", 0), ("M", 1), ("C", 0), ("Y", 1), ("M", 2), ("C", 1), ("Y", 2), ("C", 2),
    ("M", 3), ("C", 3), ("Y", 3), ("F", 0), ("Z", 0), ("F", 1), ("Z", 1), ("Z", 2), ("F", 2), ("F", 3),
    ("Z", 3),
)


def kernel(
    sizes,
    values_in, keys_in, queries_in, forget_in, skip_in, cot_in,
    mixed_out, gv_out, gbc_out,
    values_ref, keys_ref, queries_ref, forget_ref, skip_ref, cot_ref,
    mixed_ref, gv_ref, gbc_ref,
    e_head, e_tail, mix_acc, gv_acc, bc_acc,
    dx_send, dx_recv, dz_send, dz_recv,
    map_send, maps, slice_send, slices, states, states_out,
    zin_send, zin_recv, zout_send, zout_recv, cross_send, cross,
    grads, pair_recv, sums_send, sums_recv,
    send_sem, recv_sem, load_sem, round_sem, write_sem,
):
    groups, peers = sizes
    seqs, rows, wide = values_ref.shape
    heads = forget_ref.shape[1]
    width = wide // heads
    state = keys_ref.shape[2]
    lanes = wide // GROUP
    piece = state // groups
    depth = groups // 2
    part = rows // peers

    me_seq = lax.axis_index("seq")
    me_head = lax.axis_index("head")
    me_x = lax.rem(me_seq, GROUP)
    me_g = me_seq // GROUP
    me_y, me_z = me_g // depth, lax.rem(me_g, depth)

    loads = [
        pltpu.make_async_copy(src, dst, load_sem.at[n])
        for n, (src, dst) in enumerate(
            (
                (forget_in, forget_ref), (queries_in, queries_ref), (cot_in, cot_ref),
                (keys_in, keys_ref), (values_in, values_ref), (skip_in, skip_ref),
            )
        )
    ]
    for load in loads:
        load.start()

    def at_x(x):
        return (me_g * GROUP + x, me_head)

    def at_group(g):
        return (g * GROUP + me_x, me_head)

    x_peers = [lax.rem(me_x + k, GROUP) for k in (2, 1, 3)]
    away = sorted(
        ((dy, dz) for dy in range(2) for dz in range(depth) if dy or dz),
        key=lambda d: -(d[0] + min(d[1], depth - d[1])),
    )
    z_peers = [
        lax.rem(me_y + dy, 2) * depth + lax.rem(me_z + dz, depth) for dy, dz in away
    ]
    cores = 2
    ring = peers // cores
    share = rows // cores
    me_r, me_c = me_head // cores, lax.rem(me_head, cores)
    far = sorted(
        ((dr, dx) for dr in range(ring) for dx in range(GROUP) if dr or dx),
        key=lambda d: -(2 * min(d[0], ring - d[0]) + min(d[1], GROUP - d[1])),
    )
    members = [(lax.rem(me_r + dr, ring), lax.rem(me_x + dx, GROUP)) for dr, dx in far]

    def at_member(r, x):
        return (me_g * GROUP + x, r * cores + me_c)

    def at_ring(r):
        return (me_seq, r * cores + me_c)

    def steps(size, *distances):
        return sorted({d % size for d in distances} - {0})

    def z_near(*distances):
        return [
            at_group(me_y * depth + lax.rem(me_z + d, depth)) for d in steps(depth, *distances)
        ]

    y_other = [at_group((1 - me_y) * depth + me_z)]
    core_other = (me_seq, me_r * cores + 1 - me_c)
    r_near = [at_ring(lax.rem(me_r + d, ring)) for d in steps(ring, 1, -1)]
    barrier = pltpu.get_barrier_semaphore()
    near = [at_x(x) for x in x_peers] + [core_other] + r_near + y_other + z_near(1, -1, 2, -2)
    for target in near:
        pl.semaphore_signal(barrier, 1, device_id=target, device_id_type=MESH)
    r_far = [at_ring(lax.rem(me_r + 2, ring))] if ring > 3 else []
    rounds = (z_near(2, -2) + y_other, y_other, r_near, r_far)

    def tell(n):
        for target in rounds[n]:
            pl.semaphore_signal(round_sem.at[n], 1, device_id=target, device_id_type=MESH)

    def told(n):
        if rounds[n]:
            pl.semaphore_wait(round_sem.at[n], len(rounds[n]))

    def copy(src, dst, send, recv, target):
        return pltpu.make_async_remote_copy(
            src_ref=src, dst_ref=dst, send_sem=send_sem.at[send], recv_sem=recv_sem.at[recv],
            device_id=target, device_id_type=MESH,
        )

    streams = 2 * seqs
    MAPS, PASSED, SLICES, Z_IN, Z_OUT, CROSS, PAIR, SUMS = range(2, 10)

    def slot(phase, q):
        return 2 + (phase - 2) * streams + q

    def each_total(q, g):
        return 2 + 8 * streams + (q // 2) * groups + g

    def arrived(view, at):
        copy(view, view, at, at, (me_seq, me_head)).wait_recv()

    def sent(view, at):
        copy(view, view, at, at, (me_seq, me_head)).wait_send()

    every = seqs * wide
    lane_head = iota((seqs * heads, every), 1) // width
    spread_heads = (lane_head == iota((seqs * heads, every), 0)).astype(BF16)
    row2, col2 = iota((2 * rows, 2 * rows), 0), iota((2 * rows, 2 * rows), 1)
    upto = jnp.where(
        row2 < rows,
        (lax.rem(col2, rows) <= row2).astype(F32),
        (lax.rem(col2, rows) > row2 - rows).astype(F32),
    ).astype(BF16)
    row_w, lane_w = iota((rows, wide), 0), lax.rem(iota((rows, wide), 1), width)

    loads[0].wait()
    flat = forget_ref[...].reshape(seqs * heads, rows)
    high = flat.astype(BF16)
    low = (flat - high.astype(F32)).astype(BF16)
    high, low = dot_tn(high, spread_heads), dot_tn(low, spread_heads)
    sums = dot(upto, jnp.concatenate([high, low], axis=0).astype(BF16))
    for s in range(seqs):
        cols = slice(s * wide, (s + 1) * wide)
        e_head[s] = jnp.exp(-sums[:rows, cols])
        e_tail[s] = jnp.exp(-sums[rows:, cols])
        total = jnp.exp(-sums[rows - 1 : rows, cols])
        for j in range(GROUP):
            dx_send[j, s : s + 1] = total[:, j * lanes : (j + 1) * lanes]
    dx_recv[me_x] = dx_send[me_x]

    mine = pl.ds(pl.multiple_of(me_c * share, share), share)

    def send_inputs(q):
        s, back = q // 2, 1 - q % 2
        map_ref, input_ref, scale = (
            (queries_ref, cot_ref, e_head) if back else (keys_ref, values_ref, e_tail)
        )
        map_send[q] = map_ref[s].astype(F32)
        if q == 0:
            pl.semaphore_wait(barrier, len(near))
            tell(0)
            tell(2)
            for x in x_peers:
                copy(dx_send.at[x], dx_recv.at[me_x], 0, 0, at_x(x)).start()
        for x in x_peers:
            copy(
                map_send.at[q, mine], maps.at[q, me_x, mine], MAPS, slot(MAPS, q), at_x(x)
            ).start()
        scaled = input_ref[s].astype(F32) * scale[s]
        for j in range(GROUP):
            slice_send[q, j] = scaled[:, j * lanes : (j + 1) * lanes]
        for x in x_peers:
            copy(
                slice_send.at[q, x], slices.at[q, me_x], SLICES, slot(SLICES, q), at_x(x)
            ).start()
        maps[q, me_x, mine] = map_send[q, mine]
        slices[q, me_x] = slice_send[q, me_x]

    loads[1].wait()
    loads[2].wait()
    send_inputs(0)
    for load in loads[3:]:
        load.wait()

    def local_work(s):
        own = slice(s * wide, (s + 1) * wide)
        zero = jnp.zeros((rows, wide), F32)

        def gap(keep, span):
            picked = jnp.concatenate(
                [jnp.where(keep, high[:, own], zero), jnp.where(keep, low[:, own], zero)], axis=0
            ).astype(BF16)
            return jnp.exp(-dot(span, picked))

        decay = jnp.where(lane_w <= row_w, gap(row_w > lane_w, upto[:rows]), 0.0)
        decay_t = jnp.where(lane_w >= row_w, gap(row_w <= lane_w, upto[rows:]), 0.0)
        keys, queries = keys_ref[s], queries_ref[s]
        keys2 = jnp.concatenate([keys, keys], axis=0)
        queries2 = jnp.concatenate([queries, queries], axis=0)
        copies = wide // (2 * rows)
        scores = jnp.concatenate([dot_nt(queries, keys2)] * copies, axis=1)
        scores_t = jnp.concatenate([dot_nt(keys, queries2)] * copies, axis=1)
        weights = (scores * decay).astype(BF16)
        weights_t = (scores_t * decay_t).astype(BF16)
        quad = 4 * width
        mask = (iota((quad, quad), 0) // rows == iota((quad, quad), 1) // width).astype(BF16)
        grad_sum = None
        for c in range(wide // quad):
            cols = slice(c * quad, (c + 1) * quad)
            val, cot = values_ref[s, :, cols], cot_ref[s, :, cols]
            val_diag = jnp.concatenate([val] * 4, axis=0) * mask
            cot_diag = jnp.concatenate([cot] * 4, axis=0) * mask
            skip_row = jnp.concatenate(
                [
                    jnp.broadcast_to(skip_ref[0:1, 4 * c + i : 4 * c + i + 1], (1, width))
                    for i in range(4)
                ],
                axis=1,
            )
            mix_acc[s, :, cols] = dot(weights[:, cols], val_diag) + skip_row * val.astype(F32)
            gv_acc[s, :, cols] = dot(weights_t[:, cols], cot_diag) + skip_row * cot.astype(F32)
            grad_w = dot_nt(cot, val_diag) * decay[:, cols]
            for i in range(2):
                term = grad_w[:, i * 2 * width : (i + 1) * 2 * width]
                grad_sum = term if grad_sum is None else grad_sum + term
        grad_sum = grad_sum.astype(BF16)
        bc_acc[2 * s] = dot(grad_sum, keys2)
        folded = dot_tn(grad_sum, queries)
        bc_acc[2 * s + 1] = folded[:rows] + folded[rows:]

    def decay_x(s, i):
        return dx_recv[i, s : s + 1]

    def decay_z(s, g):
        return dz_recv[g, s : s + 1]

    def pass_maps(q):
        arrived(maps.at[q, pl.ds(0, GROUP - 1), pl.ds(0, share)], slot(MAPS, q))
        view = maps.at[q, pl.ds(0, GROUP), mine]
        copy(view, view, PASSED, slot(PASSED, q), core_other).start()

    def group_total(q):
        s, back = q // 2, 1 - q % 2
        arrived(slices.at[q, pl.ds(0, GROUP - 1)], slot(SLICES, q))
        arrived(maps.at[q, pl.ds(0, GROUP), pl.ds(0, share)], slot(PASSED, q))
        weighted, weight = [None] * GROUP, None
        for i in range(GROUP) if back else range(GROUP - 1, -1, -1):
            weighted[i] = slices[q, i] if weight is None else weight * slices[q, i]
            weight = decay_x(s, i) if weight is None else weight * decay_x(s, i)
        all_maps = maps[q].reshape(GROUP * rows, state).astype(BF16)
        total = dot_tn(all_maps, jnp.concatenate(weighted, axis=0).astype(BF16))
        zin_send[q] = total.reshape(groups, piece, lanes)
        at = slot(Z_IN, q) if back else each_total(q, me_g)
        for g in z_peers:
            copy(zin_send.at[q, g], zin_recv.at[q, me_g], Z_IN, at, at_group(g)).start()
        zin_recv[q, me_g] = zin_send[q, me_g]
        for i in range(1, GROUP) if back else range(GROUP - 1):
            states[q, i] = dot_tn(maps[q, i].astype(BF16), slices[q, i].astype(BF16))

    def carry_out(q, g):
        @pl.when(me_g != g)
        def _():
            copy(
                zout_send.at[q, g], zout_recv.at[q, me_g], Z_OUT, slot(Z_OUT, q), at_group(g)
            ).start()

        @pl.when(me_g == g)
        def _():
            zout_recv[q, g] = zout_send[q, g]

    def one_total(q, g):
        @pl.when(me_g != g)
        def _():
            arrived(zin_recv.at[q, g], each_total(q, g))

    def group_scan(q):
        s, back = q // 2, 1 - q % 2
        if back:
            arrived(zin_recv.at[q, pl.ds(0, groups - 1)], slot(Z_IN, q))
        carry = jnp.zeros((piece, lanes), F32)
        for n, g in enumerate(range(groups - 1, -1, -1) if back else range(groups)):
            zout_send[q, g] = carry
            if not back:
                carry_out(q, g)
                if n < groups - 1:
                    one_total(q, g)
            if n < groups - 1:
                carry = decay_z(s, g) * carry + zin_recv[q, g]
        if back:
            for g in z_peers:
                copy(
                    zout_send.at[q, g], zout_recv.at[q, me_g], Z_OUT, slot(Z_OUT, q), at_group(g)
                ).start()
            zout_recv[q, me_g] = zout_send[q, me_g]

    def member_scan(q):
        s, back = q // 2, 1 - q % 2
        other = q - 1 if q % 2 else q + 1
        arrived(zout_recv.at[q, pl.ds(0, groups - 1)], slot(Z_OUT, q))
        order = range(GROUP - 1, -1, -1) if back else range(GROUP)
        carry = zout_recv[q].reshape(state, lanes)
        carried = [None] * GROUP
        for n, i in enumerate(order):
            carried[i] = carry.astype(BF16)
            states_out[q, i] = carried[i]
            grad = dot_nt(slices[other, i].astype(BF16), carried[i])
            grad = grad.reshape(ring, cores, part, state)
            for c in range(cores):
                grads[q, c, :, i] = grad[:, c]
            if n < GROUP - 1:
                carry = decay_x(s, i) * carry + states[q, i]
        own = bc_acc[2 * s + back].reshape(ring, cores, part, state)
        for c in range(cores):
            grads[q, c, :, me_x] = grads[q, c, :, me_x] + own[:, c]
        copy(grads.at[q, 1 - me_c], pair_recv.at[q], PAIR, slot(PAIR, q), core_other).start()

    def send_cross(q):
        other = q - 1 if q % 2 else q + 1
        for i in range(GROUP):
            cross_send[q, i] = dot(maps[other, i].astype(BF16), states_out[q, i])
        for x in x_peers:
            copy(
                cross_send.at[q, x], cross.at[q, me_x], CROSS, slot(CROSS, q), at_x(x)
            ).start()
        cross[q, me_x] = cross_send[q, me_x]

    def sum_pair(q):
        arrived(pair_recv.at[q], slot(PAIR, q))
        sums_send[q] = grads[q, me_c] + pair_recv[q]
        me = me_r * GROUP + me_x
        for r, x in members:
            copy(
                sums_send.at[q, r, x], sums_recv.at[q, me], SUMS, slot(SUMS, q), at_member(r, x)
            ).start()
        sums_recv[q, me] = sums_send[q, me_r, me_x]

    def sum_all(q):
        s, back = q // 2, 1 - q % 2
        arrived(sums_recv.at[q, pl.ds(0, len(members))], slot(SUMS, q))
        total = sums_recv[q, 0]
        for n in range(1, ring * GROUP):
            total = total + sums_recv[q, n]
        gbc_ref[1 - back, s] = total
        written.append(
            pltpu.make_async_copy(
                gbc_ref.at[1 - back, s], gbc_out.at[1 - back, s], write_sem.at[streams + q]
            )
        )
        written[-1].start()

    written = []

    def finish(q):
        s, back = q // 2, 1 - q % 2
        arrived(cross.at[q, pl.ds(0, GROUP - 1)], slot(CROSS, q))
        terms = jnp.concatenate([cross[q, j] for j in range(GROUP)], axis=1)
        if back:
            gv_ref[s] = (gv_acc[s] + e_tail[s] * terms).astype(BF16)
        else:
            mixed_ref[s] = (mix_acc[s] + e_head[s] * terms).astype(BF16)
        source, result = (gv_ref, gv_out) if back else (mixed_ref, mixed_out)
        written.append(pltpu.make_async_copy(source.at[s], result.at[s], write_sem.at[q]))
        written[-1].start()

    def hear_near():
        told(0)
        tell(1)
        told(2)
        tell(3)

    def group_decays():
        arrived(dx_recv.at[pl.ds(0, GROUP - 1)], 0)
        product = dx_recv[0]
        for i in range(1, GROUP):
            product = product * dx_recv[i]
        dz_send[...] = product
        dz_recv[me_g] = product
        told(1)
        for g in z_peers:
            copy(dz_send, dz_recv.at[me_g], 1, 1, at_group(g)).start()

    def all_decays():
        arrived(dz_recv.at[pl.ds(0, groups - 1)], 1)

    work = {
        "I": send_inputs, "B": pass_maps, "T": group_total, "S": group_scan, "M": member_scan, "Y": send_cross,
        "C": sum_pair,
        "Z": sum_all, "F": finish, "L": local_work,
        "K": lambda n: (hear_near, group_decays, lambda: told(3))[n](), "D": lambda _: all_decays(),
    }

    def run(order):
        for kind, at in order:
            work[kind](at)

    run(ORDER)
    for q in range(1, streams, 2):
        one_total(q, groups - 1)
    sent(dx_send.at[pl.ds(0, GROUP - 1)], 0)
    sent(dz_recv.at[pl.ds(0, groups - 1)], 1)
    sent(maps.at[:, pl.ds(0, GROUP - 1), pl.ds(0, share)], MAPS)
    sent(maps.at[:, :, pl.ds(0, share)], PASSED)
    sent(slices.at[:, pl.ds(0, GROUP - 1)], SLICES)
    sent(zin_recv.at[:, pl.ds(0, groups - 1)], Z_IN)
    sent(zout_recv.at[:, pl.ds(0, groups - 1)], Z_OUT)
    sent(cross.at[:, pl.ds(0, GROUP - 1)], CROSS)
    sent(pair_recv, PAIR)
    sent(sums_recv.at[:, pl.ds(0, len(members))], SUMS)
    for result in written:
        result.wait()


def write_out(*refs):
    count = len(refs) // 2
    sources, results, sem = refs[:count], refs[count : 2 * count], refs[-1]
    copies = [
        pltpu.make_async_copy(a, b, sem.at[n]) for n, (a, b) in enumerate(zip(sources, results))
    ]
    for each in copies:
        each.start()
    for each in copies:
        each.wait()


def solution(mesh):
    blocks, peers = mesh.shape["seq"], mesh.shape["head"]
    groups = blocks // GROUP

    def shards(values, keys_b, queries_c, forget, skip, cotangent):
        seqs, rows, wide = values.shape
        state = keys_b.shape[-1]
        streams = 2 * seqs
        lanes, piece, part = wide // GROUP, state // groups, rows // peers
        anywhere = pl.BlockSpec(memory_space=pl.ANY)
        args = (values, keys_b, queries_c, forget, skip.reshape(1, -1), cotangent)
        results = (
            (values.shape, BF16),
            (values.shape, BF16),
            ((2, seqs, part, state), F32),
        )
        inner = pl.pallas_call(
            functools.partial(kernel, (groups, peers)),
            out_shape=tuple(pltpu.VMEM(*r) for r in results),
            in_specs=[anywhere] * len(args),
            out_specs=(anywhere,) * len(results),
            scratch_shapes=[pltpu.VMEM(a.shape, a.dtype) for a in args]
            + [pltpu.VMEM(*r) for r in results]
            + [
                *[pltpu.VMEM((seqs, rows, wide), F32)] * 4,
                pltpu.VMEM((2 * seqs, rows, state), F32),
                *[pltpu.VMEM((GROUP, seqs, lanes), F32)] * 2,
                pltpu.VMEM((seqs, lanes), F32),
                pltpu.VMEM((groups, seqs, lanes), F32),
                pltpu.VMEM((streams, rows, state), F32),
                pltpu.VMEM((streams, GROUP, rows, state), F32),
                *[pltpu.VMEM((streams, GROUP, rows, lanes), F32)] * 2,
                pltpu.VMEM((streams, GROUP, state, lanes), F32),
                pltpu.VMEM((streams, GROUP, state, lanes), BF16),
                *[pltpu.VMEM((streams, groups, piece, lanes), F32)] * 4,
                *[pltpu.VMEM((streams, GROUP, rows, lanes), F32)] * 2,
                pltpu.VMEM((streams, 2, peers // 2, GROUP, part, state), F32),
                *[pltpu.VMEM((streams, peers // 2, GROUP, part, state), F32)] * 2,
                pltpu.VMEM((streams, peers // 2 * GROUP, part, state), F32),
                pltpu.SemaphoreType.DMA((10,)),
                pltpu.SemaphoreType.DMA((2 + 8 * streams + seqs * groups,)),
                pltpu.SemaphoreType.DMA((len(args),)),
                pltpu.SemaphoreType.REGULAR((4,)),
                pltpu.SemaphoreType.DMA((2 * streams,)),
            ],
            compiler_params=pltpu.CompilerParams(collective_id=0, has_side_effects=True),
        )(*args)
        return pl.pallas_call(
            write_out,
            out_shape=tuple(jax.ShapeDtypeStruct(*r) for r in results),
            in_specs=[anywhere] * len(results),
            out_specs=(anywhere,) * len(results),
            scratch_shapes=[pltpu.SemaphoreType.DMA((len(results),))],
        )(*[pltpu.with_memory_space_constraint(x, pltpu.VMEM) for x in inner])

    in_specs = (
        P(None, "seq", "head"),
        P(None, "seq", None),
        P(None, "seq", None),
        P(None, "head", "seq"),
        P("head"),
        P(None, "seq", "head"),
    )
    out_specs = (
        P(None, "seq", "head"),
        P(None, "seq", "head"),
        P(None, None, ("seq", "head"), None),
    )
    return jax.shard_map(shards, mesh=mesh, in_specs=in_specs, out_specs=out_specs, check_vma=False)
```

```python
import functools

import jax
import jax.numpy as jnp
from jax import lax
from jax.experimental import pallas as pl
from jax.experimental.pallas import tpu as pltpu
from jax.sharding import PartitionSpec as P

MESH = pl.DeviceIdType.MESH
EARLY = 4
GROUP = 4
F32 = jnp.float32
BF16 = jnp.bfloat16


def dot(a, b):
    return lax.dot_general(a, b, (((1,), (0,)), ((), ())), preferred_element_type=F32)


def dot_nt(a, b):
    return lax.dot_general(a, b, (((1,), (1,)), ((), ())), preferred_element_type=F32)


def dot_tn(a, b):
    return lax.dot_general(a, b, (((0,), (0,)), ((), ())), preferred_element_type=F32)


def iota(shape, dim):
    return lax.broadcasted_iota(jnp.int32, shape, dim)


ORDER = (
    ("K", 0), ("I", 1), ("B", 0), ("I", 2), ("K", 1), ("T", 0), ("B", 1), ("I", 3), ("L", 0), ("T", 1),
    ("B", 2), ("L", 1), ("T", 2), ("B", 3), ("D", 0), ("S", 0), ("T", 3), ("S", 1), ("S", 2), ("K", 2),
    ("M", 0), ("S", 3), ("C", 0), ("Y", 0), ("M", 1), ("Y", 1), ("C", 1), ("M", 2), ("Y", 2), ("C", 2),
    ("M", 3), ("C", 3), ("Y", 3), ("F", 0), ("Z", 0), ("F", 1), ("Z", 1), ("Z", 2), ("F", 2), ("F", 3),
    ("Z", 3),
)


def kernel(
    sizes,
    values_in, keys_in, queries_in, forget_in, skip_in, cot_in,
    mixed_out, gv_out, gbc_out,
    values_ref, keys_ref, queries_ref, forget_ref, skip_ref, cot_ref,
    mixed_ref, gv_ref, gbc_ref,
    e_head, e_tail, mix_acc, gv_acc, bc_acc,
    dx_send, dx_recv, dz_send, dz_recv,
    map_send, maps, slice_send, slices, states, states_out,
    zin_send, zin_recv, zout_send, zout_recv, cross_send, cross,
    grads, pair_recv, sums_send, sums_recv,
    send_sem, recv_sem, load_sem, round_sem, write_sem,
):
    groups, peers = sizes
    seqs, rows, wide = values_ref.shape
    heads = forget_ref.shape[1]
    width = wide // heads
    state = keys_ref.shape[2]
    lanes = wide // GROUP
    piece = state // groups
    depth = groups // 2
    part = rows // peers

    me_seq = lax.axis_index("seq")
    me_head = lax.axis_index("head")
    me_x = lax.rem(me_seq, GROUP)
    me_g = me_seq // GROUP
    me_y, me_z = me_g // depth, lax.rem(me_g, depth)

    loads = [
        pltpu.make_async_copy(src, dst, load_sem.at[n])
        for n, (src, dst) in enumerate(
            (
                (forget_in, forget_ref), (queries_in, queries_ref), (cot_in, cot_ref),
                (keys_in, keys_ref), (values_in, values_ref), (skip_in, skip_ref),
            )
        )
    ]
    for load in loads:
        load.start()

    def at_x(x):
        return (me_g * GROUP + x, me_head)

    def at_group(g):
        return (g * GROUP + me_x, me_head)

    x_peers = [lax.rem(me_x + k, GROUP) for k in (2, 1, 3)]
    away = sorted(
        ((dy, dz) for dy in range(2) for dz in range(depth) if dy or dz),
        key=lambda d: -(d[0] + min(d[1], depth - d[1])),
    )
    z_peers = [
        lax.rem(me_y + dy, 2) * depth + lax.rem(me_z + dz, depth) for dy, dz in away
    ]
    cores = 2
    ring = peers // cores
    share = rows // cores
    me_r, me_c = me_head // cores, lax.rem(me_head, cores)
    far = sorted(
        ((dr, dx) for dr in range(ring) for dx in range(GROUP) if dr or dx),
        key=lambda d: -(2 * min(d[0], ring - d[0]) + min(d[1], GROUP - d[1])),
    )
    members = [(lax.rem(me_r + dr, ring), lax.rem(me_x + dx, GROUP)) for dr, dx in far]

    def at_member(r, x):
        return (me_g * GROUP + x, r * cores + me_c)

    def at_ring(r):
        return (me_seq, r * cores + me_c)

    def steps(size, *distances):
        return sorted({d % size for d in distances} - {0})

    def z_near(*distances):
        return [
            at_group(me_y * depth + lax.rem(me_z + d, depth)) for d in steps(depth, *distances)
        ]

    y_other = [at_group((1 - me_y) * depth + me_z)]
    core_other = (me_seq, me_r * cores + 1 - me_c)
    r_near = [at_ring(lax.rem(me_r + d, ring)) for d in steps(ring, 1, -1)]
    barrier = pltpu.get_barrier_semaphore()
    near = [at_x(x) for x in x_peers] + [core_other] + r_near + y_other + z_near(1, -1, 2, -2)
    for target in near:
        pl.semaphore_signal(barrier, 1, device_id=target, device_id_type=MESH)
    r_far = [at_ring(lax.rem(me_r + 2, ring))] if ring > 3 else []
    rounds = (z_near(2, -2) + y_other, y_other, r_near, r_far)

    def tell(n):
        for target in rounds[n]:
            pl.semaphore_signal(round_sem.at[n], 1, device_id=target, device_id_type=MESH)

    def told(n):
        if rounds[n]:
            pl.semaphore_wait(round_sem.at[n], len(rounds[n]))

    def copy(src, dst, send, recv, target):
        return pltpu.make_async_remote_copy(
            src_ref=src, dst_ref=dst, send_sem=send_sem.at[send], recv_sem=recv_sem.at[recv],
            device_id=target, device_id_type=MESH,
        )

    streams = 2 * seqs
    MAPS, PASSED, SLICES, Z_IN, Z_OUT, CROSS, PAIR, SUMS = range(2, 10)

    def slot(phase, q):
        return 2 + (phase - 2) * streams + q

    def each_total(q, g):
        return 2 + 8 * streams + (q // 2) * groups + g

    def arrived(view, at):
        copy(view, view, at, at, (me_seq, me_head)).wait_recv()

    def sent(view, at):
        copy(view, view, at, at, (me_seq, me_head)).wait_send()

    every = seqs * wide
    lane_head = iota((seqs * heads, every), 1) // width
    spread_heads = (lane_head == iota((seqs * heads, every), 0)).astype(BF16)
    row2, col2 = iota((2 * rows, 2 * rows), 0), iota((2 * rows, 2 * rows), 1)
    upto = jnp.where(
        row2 < rows,
        (lax.rem(col2, rows) <= row2).astype(F32),
        (lax.rem(col2, rows) > row2 - rows).astype(F32),
    ).astype(BF16)
    row_w, lane_w = iota((rows, wide), 0), lax.rem(iota((rows, wide), 1), width)

    loads[0].wait()
    flat = forget_ref[...].reshape(seqs * heads, rows)
    high = flat.astype(BF16)
    low = (flat - high.astype(F32)).astype(BF16)
    high, low = dot_tn(high, spread_heads), dot_tn(low, spread_heads)
    sums = dot(upto, jnp.concatenate([high, low], axis=0).astype(BF16))
    for s in range(seqs):
        cols = slice(s * wide, (s + 1) * wide)
        e_head[s] = jnp.exp(-sums[:rows, cols])
        e_tail[s] = jnp.exp(-sums[rows:, cols])
        total = jnp.exp(-sums[rows - 1 : rows, cols])
        for j in range(GROUP):
            dx_send[j, s : s + 1] = total[:, j * lanes : (j + 1) * lanes]
    dx_recv[me_x] = dx_send[me_x]

    mine = pl.ds(pl.multiple_of(me_c * share, share), share)

    def send_inputs(q):
        s, back = q // 2, 1 - q % 2
        map_ref, input_ref, scale = (
            (queries_ref, cot_ref, e_head) if back else (keys_ref, values_ref, e_tail)
        )
        map_send[q] = map_ref[s].astype(F32)
        if q == 0:
            pl.semaphore_wait(barrier, len(near))
            tell(0)
            tell(2)
            for x in x_peers:
                copy(dx_send.at[x], dx_recv.at[me_x], 0, 0, at_x(x)).start()
        for x in x_peers:
            copy(
                map_send.at[q, mine], maps.at[q, me_x, mine], MAPS, slot(MAPS, q), at_x(x)
            ).start()
        scaled = input_ref[s].astype(F32) * scale[s]
        for j in range(GROUP):
            slice_send[q, j] = scaled[:, j * lanes : (j + 1) * lanes]
        for x in x_peers:
            copy(
                slice_send.at[q, x], slices.at[q, me_x], SLICES, slot(SLICES, q), at_x(x)
            ).start()
        maps[q, me_x, mine] = map_send[q, mine]
        slices[q, me_x] = slice_send[q, me_x]

    loads[1].wait()
    loads[2].wait()
    send_inputs(0)
    for load in loads[3:]:
        load.wait()

    def local_work(s):
        own = slice(s * wide, (s + 1) * wide)
        zero = jnp.zeros((rows, wide), F32)

        def gap(keep, span):
            picked = jnp.concatenate(
                [jnp.where(keep, high[:, own], zero), jnp.where(keep, low[:, own], zero)], axis=0
            ).astype(BF16)
            return jnp.exp(-dot(span, picked))

        decay = jnp.where(lane_w <= row_w, gap(row_w > lane_w, upto[:rows]), 0.0)
        decay_t = jnp.where(lane_w >= row_w, gap(row_w <= lane_w, upto[rows:]), 0.0)
        keys, queries = keys_ref[s], queries_ref[s]
        keys2 = jnp.concatenate([keys, keys], axis=0)
        queries2 = jnp.concatenate([queries, queries], axis=0)
        copies = wide // (2 * rows)
        scores = jnp.concatenate([dot_nt(queries, keys2)] * copies, axis=1)
        scores_t = jnp.concatenate([dot_nt(keys, queries2)] * copies, axis=1)
        weights = (scores * decay).astype(BF16)
        weights_t = (scores_t * decay_t).astype(BF16)
        quad = 4 * width
        mask = (iota((quad, quad), 0) // rows == iota((quad, quad), 1) // width).astype(BF16)
        grad_sum = None
        for c in range(wide // quad):
            cols = slice(c * quad, (c + 1) * quad)
            val, cot = values_ref[s, :, cols], cot_ref[s, :, cols]
            val_diag = jnp.concatenate([val] * 4, axis=0) * mask
            cot_diag = jnp.concatenate([cot] * 4, axis=0) * mask
            skip_row = jnp.concatenate(
                [
                    jnp.broadcast_to(skip_ref[0:1, 4 * c + i : 4 * c + i + 1], (1, width))
                    for i in range(4)
                ],
                axis=1,
            )
            mix_acc[s, :, cols] = dot(weights[:, cols], val_diag) + skip_row * val.astype(F32)
            gv_acc[s, :, cols] = dot(weights_t[:, cols], cot_diag) + skip_row * cot.astype(F32)
            grad_w = dot_nt(cot, val_diag) * decay[:, cols]
            for i in range(2):
                term = grad_w[:, i * 2 * width : (i + 1) * 2 * width]
                grad_sum = term if grad_sum is None else grad_sum + term
        grad_sum = grad_sum.astype(BF16)
        bc_acc[2 * s] = dot(grad_sum, keys2)
        folded = dot_tn(grad_sum, queries)
        bc_acc[2 * s + 1] = folded[:rows] + folded[rows:]

    def decay_x(s, i):
        return dx_recv[i, s : s + 1]

    def decay_z(s, g):
        return dz_recv[g, s : s + 1]

    def pass_maps(q):
        arrived(maps.at[q, pl.ds(0, GROUP - 1), pl.ds(0, share)], slot(MAPS, q))
        view = maps.at[q, pl.ds(0, GROUP), mine]
        copy(view, view, PASSED, slot(PASSED, q), core_other).start()

    def group_total(q):
        s, back = q // 2, 1 - q % 2
        arrived(slices.at[q, pl.ds(0, GROUP - 1)], slot(SLICES, q))
        arrived(maps.at[q, pl.ds(0, GROUP), pl.ds(0, share)], slot(PASSED, q))
        weighted, weight = [None] * GROUP, None
        for i in range(GROUP) if back else range(GROUP - 1, -1, -1):
            weighted[i] = slices[q, i] if weight is None else weight * slices[q, i]
            weight = decay_x(s, i) if weight is None else weight * decay_x(s, i)
        all_maps = maps[q].reshape(GROUP * rows, state).astype(BF16)
        total = dot_tn(all_maps, jnp.concatenate(weighted, axis=0).astype(BF16))
        zin_send[q] = total.reshape(groups, piece, lanes)
        at = slot(Z_IN, q) if back else each_total(q, me_g)
        for g in z_peers:
            copy(zin_send.at[q, g], zin_recv.at[q, me_g], Z_IN, at, at_group(g)).start()
        zin_recv[q, me_g] = zin_send[q, me_g]
        for i in range(1, GROUP) if back else range(GROUP - 1):
            states[q, i] = dot_tn(maps[q, i].astype(BF16), slices[q, i].astype(BF16))

    def carry_out(q, g):
        @pl.when(me_g != g)
        def _():
            copy(
                zout_send.at[q, g], zout_recv.at[q, me_g], Z_OUT, slot(Z_OUT, q), at_group(g)
            ).start()

        @pl.when(me_g == g)
        def _():
            zout_recv[q, g] = zout_send[q, g]

    def late_out(q, g):
        copy(
            zout_send.at[q, g], zout_recv.at[q, me_g], Z_OUT, slot(Z_OUT, q), at_group(g)
        ).start()

    def one_total(q, g):
        @pl.when(me_g != g)
        def _():
            arrived(zin_recv.at[q, g], each_total(q, g))

    def group_scan(q):
        s, back = q // 2, 1 - q % 2
        if back:
            arrived(zin_recv.at[q, pl.ds(0, groups - 1)], slot(Z_IN, q))
        carry = jnp.zeros((piece, lanes), F32)
        for n, g in enumerate(range(groups - 1, -1, -1) if back else range(groups)):
            zout_send[q, g] = carry
            if not back:
                if g < EARLY:
                    carry_out(q, g)
                if n < groups - 1:
                    one_total(q, g)
            if n < groups - 1:
                carry = decay_z(s, g) * carry + zin_recv[q, g]
        if back:
            for g in z_peers:
                copy(
                    zout_send.at[q, g], zout_recv.at[q, me_g], Z_OUT, slot(Z_OUT, q), at_group(g)
                ).start()
            zout_recv[q, me_g] = zout_send[q, me_g]
        else:
            for g in z_peers:
                pl.when(g >= EARLY)(functools.partial(late_out, q, g))

            @pl.when(me_g >= EARLY)
            def _():
                zout_recv[q, me_g] = zout_send[q, me_g]

    def member_scan(q):
        s, back = q // 2, 1 - q % 2
        other = q - 1 if q % 2 else q + 1
        arrived(zout_recv.at[q, pl.ds(0, groups - 1)], slot(Z_OUT, q))
        order = range(GROUP - 1, -1, -1) if back else range(GROUP)
        carry = zout_recv[q].reshape(state, lanes)
        carried = [None] * GROUP
        for n, i in enumerate(order):
            carried[i] = carry.astype(BF16)
            states_out[q, i] = carried[i]
            grad = dot_nt(slices[other, i].astype(BF16), carried[i])
            grad = grad.reshape(ring, cores, part, state)
            for c in range(cores):
                grads[q, c, :, i] = grad[:, c]
            if n < GROUP - 1:
                carry = decay_x(s, i) * carry + states[q, i]
        own = bc_acc[2 * s + back].reshape(ring, cores, part, state)
        for c in range(cores):
            grads[q, c, :, me_x] = grads[q, c, :, me_x] + own[:, c]
        copy(grads.at[q, 1 - me_c], pair_recv.at[q], PAIR, slot(PAIR, q), core_other).start()

    def send_cross(q):
        other = q - 1 if q % 2 else q + 1
        for i in range(GROUP):
            cross_send[q, i] = dot(maps[other, i].astype(BF16), states_out[q, i])
        for x in x_peers:
            copy(
                cross_send.at[q, x], cross.at[q, me_x], CROSS, slot(CROSS, q), at_x(x)
            ).start()
        cross[q, me_x] = cross_send[q, me_x]

    def sum_pair(q):
        arrived(pair_recv.at[q], slot(PAIR, q))
        sums_send[q] = grads[q, me_c] + pair_recv[q]
        me = me_r * GROUP + me_x
        for r, x in members:
            copy(
                sums_send.at[q, r, x], sums_recv.at[q, me], SUMS, slot(SUMS, q), at_member(r, x)
            ).start()
        sums_recv[q, me] = sums_send[q, me_r, me_x]

    def sum_all(q):
        s, back = q // 2, 1 - q % 2
        arrived(sums_recv.at[q, pl.ds(0, len(members))], slot(SUMS, q))
        total = sums_recv[q, 0]
        for n in range(1, ring * GROUP):
            total = total + sums_recv[q, n]
        gbc_ref[1 - back, s] = total
        written.append(
            pltpu.make_async_copy(
                gbc_ref.at[1 - back, s], gbc_out.at[1 - back, s], write_sem.at[streams + q]
            )
        )
        written[-1].start()

    written = []

    def finish(q):
        s, back = q // 2, 1 - q % 2
        arrived(cross.at[q, pl.ds(0, GROUP - 1)], slot(CROSS, q))
        terms = jnp.concatenate([cross[q, j] for j in range(GROUP)], axis=1)
        if back:
            gv_ref[s] = (gv_acc[s] + e_tail[s] * terms).astype(BF16)
        else:
            mixed_ref[s] = (mix_acc[s] + e_head[s] * terms).astype(BF16)
        source, result = (gv_ref, gv_out) if back else (mixed_ref, mixed_out)
        written.append(pltpu.make_async_copy(source.at[s], result.at[s], write_sem.at[q]))
        written[-1].start()

    def hear_near():
        told(0)
        tell(1)
        told(2)
        tell(3)

    def group_decays():
        arrived(dx_recv.at[pl.ds(0, GROUP - 1)], 0)
        product = dx_recv[0]
        for i in range(1, GROUP):
            product = product * dx_recv[i]
        dz_send[...] = product
        dz_recv[me_g] = product
        told(1)
        for g in z_peers:
            copy(dz_send, dz_recv.at[me_g], 1, 1, at_group(g)).start()

    def all_decays():
        arrived(dz_recv.at[pl.ds(0, groups - 1)], 1)

    work = {
        "I": send_inputs, "B": pass_maps, "T": group_total, "S": group_scan, "M": member_scan, "Y": send_cross,
        "C": sum_pair,
        "Z": sum_all, "F": finish, "L": local_work,
        "K": lambda n: (hear_near, group_decays, lambda: told(3))[n](), "D": lambda _: all_decays(),
    }

    def run(order):
        for kind, at in order:
            work[kind](at)

    run(ORDER)
    for q in range(1, streams, 2):
        one_total(q, groups - 1)
    sent(dx_send.at[pl.ds(0, GROUP - 1)], 0)
    sent(dz_recv.at[pl.ds(0, groups - 1)], 1)
    sent(maps.at[:, pl.ds(0, GROUP - 1), pl.ds(0, share)], MAPS)
    sent(maps.at[:, :, pl.ds(0, share)], PASSED)
    sent(slices.at[:, pl.ds(0, GROUP - 1)], SLICES)
    sent(zin_recv.at[:, pl.ds(0, groups - 1)], Z_IN)
    sent(zout_recv.at[:, pl.ds(0, groups - 1)], Z_OUT)
    sent(cross.at[:, pl.ds(0, GROUP - 1)], CROSS)
    sent(pair_recv, PAIR)
    sent(sums_recv.at[:, pl.ds(0, len(members))], SUMS)
    for result in written:
        result.wait()


def write_out(*refs):
    count = len(refs) // 2
    sources, results, sem = refs[:count], refs[count : 2 * count], refs[-1]
    copies = [
        pltpu.make_async_copy(a, b, sem.at[n]) for n, (a, b) in enumerate(zip(sources, results))
    ]
    for each in copies:
        each.start()
    for each in copies:
        each.wait()


def solution(mesh):
    blocks, peers = mesh.shape["seq"], mesh.shape["head"]
    groups = blocks // GROUP

    def shards(values, keys_b, queries_c, forget, skip, cotangent):
        seqs, rows, wide = values.shape
        state = keys_b.shape[-1]
        streams = 2 * seqs
        lanes, piece, part = wide // GROUP, state // groups, rows // peers
        anywhere = pl.BlockSpec(memory_space=pl.ANY)
        args = (values, keys_b, queries_c, forget, skip.reshape(1, -1), cotangent)
        results = (
            (values.shape, BF16),
            (values.shape, BF16),
            ((2, seqs, part, state), F32),
        )
        inner = pl.pallas_call(
            functools.partial(kernel, (groups, peers)),
            out_shape=tuple(pltpu.VMEM(*r) for r in results),
            in_specs=[anywhere] * len(args),
            out_specs=(anywhere,) * len(results),
            scratch_shapes=[pltpu.VMEM(a.shape, a.dtype) for a in args]
            + [pltpu.VMEM(*r) for r in results]
            + [
                *[pltpu.VMEM((seqs, rows, wide), F32)] * 4,
                pltpu.VMEM((2 * seqs, rows, state), F32),
                *[pltpu.VMEM((GROUP, seqs, lanes), F32)] * 2,
                pltpu.VMEM((seqs, lanes), F32),
                pltpu.VMEM((groups, seqs, lanes), F32),
                pltpu.VMEM((streams, rows, state), F32),
                pltpu.VMEM((streams, GROUP, rows, state), F32),
                *[pltpu.VMEM((streams, GROUP, rows, lanes), F32)] * 2,
                pltpu.VMEM((streams, GROUP, state, lanes), F32),
                pltpu.VMEM((streams, GROUP, state, lanes), BF16),
                *[pltpu.VMEM((streams, groups, piece, lanes), F32)] * 4,
                *[pltpu.VMEM((streams, GROUP, rows, lanes), F32)] * 2,
                pltpu.VMEM((streams, 2, peers // 2, GROUP, part, state), F32),
                *[pltpu.VMEM((streams, peers // 2, GROUP, part, state), F32)] * 2,
                pltpu.VMEM((streams, peers // 2 * GROUP, part, state), F32),
                pltpu.SemaphoreType.DMA((10,)),
                pltpu.SemaphoreType.DMA((2 + 8 * streams + seqs * groups,)),
                pltpu.SemaphoreType.DMA((len(args),)),
                pltpu.SemaphoreType.REGULAR((4,)),
                pltpu.SemaphoreType.DMA((2 * streams,)),
            ],
            compiler_params=pltpu.CompilerParams(collective_id=0, has_side_effects=True),
        )(*args)
        return pl.pallas_call(
            write_out,
            out_shape=tuple(jax.ShapeDtypeStruct(*r) for r in results),
            in_specs=[anywhere] * len(results),
            out_specs=(anywhere,) * len(results),
            scratch_shapes=[pltpu.SemaphoreType.DMA((len(results),))],
        )(*[pltpu.with_memory_space_constraint(x, pltpu.VMEM) for x in inner])

    in_specs = (
        P(None, "seq", "head"),
        P(None, "seq", None),
        P(None, "seq", None),
        P(None, "head", "seq"),
        P("head"),
        P(None, "seq", "head"),
    )
    out_specs = (
        P(None, "seq", "head"),
        P(None, "seq", "head"),
        P(None, None, ("seq", "head"), None),
    )
    return jax.shard_map(shards, mesh=mesh, in_specs=in_specs, out_specs=out_specs, check_vma=False)
```
